32 devices in a mesh: ep: 8 (over z, x), tp: 4 (over y, core).
Axes of the slice: x: 2, y: 2, z: 4, core: 2. Of those that a mesh axis runs over, the one named last changes fastest.
Arguments:
- tokens: bfloat16 [2, 128, 4096], P(None, 'ep'), may hold values from -6 to 6
- route_ids: int32 [2, 128, 8], P(None, 'ep'), may hold values from 0 to 15, all different within a row; in each aligned block of 16 rows (0 to 15, 16 to 31, ..., all dimensions but the last counted through in order) at most 10 rows name the same one
- route_weights: float32 [2, 128, 8], P(None, 'ep'), may hold values from 0.1 to 0.4
- train_map: int32 [64], replicated, may hold values from 0 to 63, each once
- serve_place: int32 [64], replicated, may hold values from 0 to 15, as said below
- train_gate: bfloat16 [64, 1024, 1536], P('ep', None, 'tp'), may hold values from -0.09375 to 0.09375
- train_up: bfloat16 [64, 1024, 1536], P('ep', None, 'tp'), may hold values from -0.09375 to 0.09375
- train_down: bfloat16 [64, 1024, 1536], P('ep', None, 'tp'), may hold values from -0.15625 to 0.15625
Outputs:
- serve_gate: bfloat16 [64, 4096, 1536], P('ep', None, 'tp')
- serve_up: bfloat16 [64, 4096, 1536], P('ep', None, 'tp')
- serve_down: bfloat16 [64, 4096, 1536], P('ep', None, 'tp')
- moe_out: bfloat16 [2, 128, 4096], P(None, 'ep', 'tp')
The draws below stay inside these ranges and needn't reach their ends.
Inputs may be any that keep to these rules, and one draw needn't show every extreme that they name: `route_ids`: each row names 8 different experts; in each aligned block of 16 rows (one index of ep in one step) no expert is named by more than 10 rows. `train_map`: each trainer slot holds a different piece; piece q is part q % 4 of expert q // 4. `serve_place`: every expert occupies two or more serving slots, and some expert exactly two.
All inputs are finite; a program needn't handle non-finite values.
Results may differ from the reference program's by a relative error of at most 0.012.
Values may be sent and summed in bfloat16 or wider, within the bound.
A program may use at most 256 MiB of HBM per device.

```python
import math
import jax
import jax.numpy as jnp
import numpy as np
from jax import lax

D = 4096
FF = 1536
TOPK = 8
EXPERTS = 16
SLOTS = 64
STEPS = 2
TOK_DEV = 16
PARTS_SIZE = 4
QUARTER = 384
TOKENS = 128
MOST = 10
N_EP = 8


def draw_serve_place(key, part):
    key_spare = jax.random.fold_in(key, 101)
    key_first = jax.random.fold_in(key, 202)
    key_second = jax.random.fold_in(key, 303)
    key_shuffle = jax.random.fold_in(key, 404)
    initial = jnp.arange(2 * EXPERTS, dtype=jnp.int32) % EXPERTS
    spare_expert = jax.random.randint(key_spare, (), 0, EXPERTS, dtype=jnp.int32)
    extra_slots = SLOTS - 2 * EXPERTS
    first_factor = jax.random.randint(key_first, (extra_slots,), 0, EXPERTS - 1, dtype=jnp.int32)
    second_factor = jax.random.randint(key_second, (extra_slots,), 0, EXPERTS - 1, dtype=jnp.int32)
    offset = first_factor * second_factor // (EXPERTS - 1)
    extra_experts = (spare_expert + 1 + offset) % EXPERTS
    combined = jnp.concatenate([initial, extra_experts.astype(jnp.int32)])
    shuffle = jax.random.permutation(key_shuffle, SLOTS)
    return combined[shuffle].astype(jnp.int32)


def levels(stream_key, shape, cuts, smallest, high):
    def one(position, shards_of):
        heights = jax.random.uniform(jax.random.fold_in(jax.random.fold_in(stream_key, 6), position), (shards_of,), jnp.float32, smallest / len(cuts), high / len(cuts))
        return jnp.repeat(jnp.exp(heights), shape[position] // shards_of).reshape((-1,) + (1,) * (len(shape) - position - 1))

    loudness = one(*cuts[0])
    for cut in cuts[1:]:
        loudness = loudness * one(*cut)
    return loudness


def assign_block(rng, own, number, rows, count, top, reach, slope):
    ranking = jax.random.permutation(rng, count)
    crowded, common = shares(count, rows * top, reach, slope, True), shares(count, rows * top, reach, slope, False)
    places = jnp.arange(count)

    def named(tallies, rotation):
        used = int((tallies > 0).sum())
        fixed = max(1, used // 4)
        moved = fixed + (places - fixed + rotation * (used - fixed)) % max(1, count - fixed)
        return jnp.zeros((count,), jnp.int32).at[ranking[jnp.where(places < fixed, places, moved)]].set(jnp.asarray(tallies, jnp.int32))

    tallies = jnp.where(number % 4 == 0, named(crowded, number // 4), named(common, number - number // 4 - 1))
    mixed = jax.random.permutation(jax.random.fold_in(own, 3), count)
    donor, taker = mixed[0:count // 2 * 2:2], mixed[1:count // 2 * 2:2]
    slack = jnp.minimum(tallies[donor] - 1, reach - tallies[taker]) // 2
    slack = jnp.where((donor == ranking[0]) | (taker == ranking[0]) | (tallies[taker] == 0), 0, jnp.maximum(slack, 0))
    moved = jax.random.randint(jax.random.fold_in(own, 4), (count // 2,), 0, 1 << 20) % (slack + 1)
    tallies = tallies.at[donor].add(-moved).at[taker].add(moved)
    members = jnp.searchsorted(jnp.cumsum(tallies), jnp.arange(rows * top), side="right").astype(jnp.int32)
    grid = members.reshape(top, rows).T
    grid = grid[jax.random.permutation(jax.random.fold_in(own, 1), rows)]
    rotation = jax.random.randint(jax.random.fold_in(own, 2), (rows, 1), 0, top)
    return jnp.take_along_axis(grid, (jnp.arange(top)[None, :] + rotation) % top, axis=1)


def shares(count, total, bound, lean, full):
    weights = [(1 << 20) // math.isqrt(grade ** lean) + 1 for grade in range(1, count + 1)]
    largest = bound if full else min(bound, max(-(-total // count), total * weights[0] // sum(weights)))
    least = 1 if total - largest >= count - 1 else 0
    given, spare = [largest] + [least] * (count - 1), total - largest - least * (count - 1)
    while spare > 0:
        movable = [i for i in range(1, count) if given[i] < largest] or [i for i in range(1, count) if given[i] < bound]
        pool, budget = sum([weights[i] for i in movable]), spare
        for i in movable:
            more = min(bound - given[i], max(1, budget * weights[i] // pool), spare)
            given[i] = given[i] + more
            spare = spare - more
    return np.array(given)


def scatter_about(own_key, shape, spread, limit, cuts=(), kind=jnp.bfloat16):
    factor_of = levels(own_key, shape, cuts, -0.22, 0.18) if cuts else 1.0
    result = jax.random.normal(own_key, shape, jnp.float32) * spread * factor_of
    return jnp.minimum(jnp.maximum(result, -limit), limit).astype(kind)


def setup_inputs(seed: int = 0) -> dict:
    key_list = jax.random.split(jax.random.key(seed), 9)
    tokens = scatter_about(key_list[0], (STEPS, TOKENS, D), 1.0, 6.0, ((1, 8),))
    route_ids_keys = jax.random.split(jax.random.fold_in(key_list[1], 1), STEPS * TOKENS // TOK_DEV)
    route_ids_turns = jax.random.permutation(jax.random.fold_in(key_list[1], 3), STEPS * TOKENS // TOK_DEV)
    route_ids = jax.vmap(lambda own, number: assign_block(jax.random.fold_in(key_list[1], 2), own, number, TOK_DEV, EXPERTS, TOPK, MOST, 2))(route_ids_keys, route_ids_turns).reshape((STEPS, TOKENS, TOPK))
    route_weights = jnp.clip(0.1 + 0.3 * jax.random.uniform(key_list[2], (STEPS, TOKENS, TOPK), jnp.float32) ** levels(key_list[2], (STEPS, TOKENS, TOPK), ((1, 8),), -0.2, 0.2), 0.1, 0.4)
    train_map = jax.random.permutation(key_list[3], SLOTS).astype(jnp.int32)
    serve_place = draw_serve_place(jax.random.fold_in(key_list[8], 71), 0)
    train_gate = scatter_about(key_list[5], (SLOTS, D // PARTS_SIZE, FF), D ** -0.5, 0.09375, ((0, 8), (2, 4)))
    train_up = scatter_about(key_list[6], (SLOTS, D // PARTS_SIZE, FF), D ** -0.5, 0.09375, ((0, 8), (2, 4)))
    train_down = scatter_about(key_list[7], (SLOTS, D // PARTS_SIZE, FF), FF ** -0.5, 0.15625, ((0, 8), (2, 4)))
    return {"tokens": tokens, "route_ids": route_ids, "route_weights": route_weights, "train_map": train_map, "serve_place": serve_place, "train_gate": train_gate, "train_up": train_up, "train_down": train_down}


def reference(tokens, route_ids, route_weights, train_map, serve_place, train_gate, train_up, train_down):
    inverse = jnp.argsort(train_map).astype(jnp.int32)
    expert_gate = train_gate[inverse].reshape(EXPERTS, D, FF)
    expert_up = train_up[inverse].reshape(EXPERTS, D, FF)
    expert_down = train_down[inverse].reshape(EXPERTS, D, FF)
    place_index = serve_place.astype(jnp.int32)
    serve_gate = expert_gate[place_index]
    serve_up = expert_up[place_index]
    serve_down = expert_down[place_index]
    capacity = min(TOKENS, N_EP * MOST)
    results = []
    for decode_step in range(STEPS):
        pair_experts = route_ids[decode_step].reshape(-1)
        pair_weights = route_weights[decode_step].reshape(-1)
        step_tokens = tokens[decode_step]

        def add_expert(expert, running):
            matches = pair_experts == expert
            ordering = jnp.argsort(jnp.where(matches, 0, 1).astype(jnp.int32), stable=True)[:capacity].astype(jnp.int32)
            valid_pair = matches[ordering]
            token_rows = (ordering // TOPK).astype(jnp.int32)
            inputs = step_tokens[token_rows]
            gate_act = jnp.dot(inputs, expert_gate[expert], preferred_element_type=jnp.float32)
            up_act = jnp.dot(inputs, expert_up[expert], preferred_element_type=jnp.float32)
            hidden = (jax.nn.silu(gate_act) * up_act).astype(jnp.bfloat16)
            down_rows = expert_down[expert]
            summed = jnp.zeros((capacity, D), jnp.float32)
            for quarter_index in range(FF // QUARTER):
                lower = quarter_index * QUARTER
                partial_value = jnp.dot(hidden[:, lower:lower + QUARTER], down_rows[:, lower:lower + QUARTER].T, preferred_element_type=jnp.float32).astype(jnp.bfloat16)
                partial_value = lax.optimization_barrier(partial_value)
                summed = summed + partial_value.astype(jnp.float32)
            expert_out = summed.astype(jnp.bfloat16)
            pair_scale = jnp.where(valid_pair, pair_weights[ordering], jnp.zeros_like(pair_weights[ordering]))
            return running.at[token_rows].add(pair_scale[:, None] * expert_out.astype(jnp.float32))

        running = lax.fori_loop(0, EXPERTS, add_expert, jnp.zeros((TOKENS, D), jnp.float32))
        results.append(running.astype(jnp.bfloat16))
    return serve_gate, serve_up, serve_down, jnp.stack(results)
```

```python
import functools

import jax
import jax.numpy as jnp
from jax import lax
from jax.experimental import pallas as pl
from jax.experimental.pallas import tpu as pltpu
from jax.sharding import PartitionSpec as P

EXPERTS = 16
MOST = 10
MESH = pl.DeviceIdType.MESH
CAPS = (34, 38)
UP_ROOM = 48


def relay_kernel(
    pairs, chunk_rows, buffers, idx_ref, t0, t1, t2, o0, o1, o2, held, whole, own, other,
    local_sem, first_send, first_recv, line_send, line_recv,
    own_sem, other_send, other_recv, stage_sem, credit_x, credit_up, credit_down,
):
    trains, outs = (t0, t1, t2), (o0, o1, o2)
    me = lax.axis_index("ep")
    z, x = lax.div(me, 2), lax.rem(me, 2)
    partner = me + 1 - 2 * x
    above, below = me + 2, me - 2
    local = t0.shape[0]
    half = t0.shape[1] // 2
    steps = half // chunk_rows
    total = len(trains) * steps
    layer = 2 * local
    picks = own.shape[1]
    recv_slots = other_recv.shape[0]
    has_up, has_down = z < pairs - 1, z > 0

    barrier = pltpu.get_barrier_semaphore()
    pl.semaphore_signal(barrier, inc=1, device_id={"ep": partner}, device_id_type=MESH)

    @pl.when(has_up)
    def _():
        pl.semaphore_signal(barrier, inc=1, device_id={"ep": above}, device_id_type=MESH)

    @pl.when(has_down)
    def _():
        pl.semaphore_signal(barrier, inc=1, device_id={"ep": below}, device_id_type=MESH)

    pl.semaphore_wait(barrier, 1 + jnp.where(has_up, 1, 0) + jnp.where(has_down, 1, 0))

    def rows_of(side, step):
        return pl.ds(pl.multiple_of(side * half + step * chunk_rows, chunk_rows), chunk_rows)

    def mine(slot):
        return held.at[slot, pl.ds(me * local, local)]

    def region(slot, level):
        return held.at[slot, pl.ds(level * layer, layer)]

    def load_copy(train, step, slot):
        return pltpu.make_async_copy(
            train.at[:, rows_of(x, step), :], mine(slot), local_sem.at[slot]
        )

    def first_copy(train, step, slot):
        return pltpu.make_async_remote_copy(
            src_ref=train.at[:, rows_of(1 - x, step), :],
            dst_ref=mine(slot),
            send_sem=first_send.at[slot],
            recv_sem=first_recv.at[slot],
            device_id={"ep": partner},
            device_id_type=MESH,
        )

    def up_copy(slot, level):
        return pltpu.make_async_remote_copy(
            src_ref=region(slot, level),
            dst_ref=region(slot, level),
            send_sem=line_send.at[slot, level],
            recv_sem=line_recv.at[slot, level],
            device_id={"ep": above},
            device_id_type=MESH,
        )

    def down_copy(slot, level):
        return pltpu.make_async_remote_copy(
            src_ref=region(slot, level),
            dst_ref=region(slot, level),
            send_sem=line_send.at[slot, level + 1],
            recv_sem=line_recv.at[slot, level],
            device_id={"ep": below},
            device_id_type=MESH,
        )

    def own_copy(out, step, stage):
        return pltpu.make_async_copy(
            own.at[stage], out.at[:, rows_of(x, step), :], own_sem.at[stage]
        )

    def other_copy(out, step, stage, recv_slot):
        return pltpu.make_async_remote_copy(
            src_ref=other.at[stage],
            dst_ref=out.at[:, rows_of(x, step), :],
            send_sem=other_send.at[stage],
            recv_sem=other_recv.at[recv_slot],
            device_id={"ep": partner},
            device_id_type=MESH,
        )

    def stage_start(n):
        slot = lax.rem(n, buffers)

        @pl.when(n >= buffers)
        def _():
            pl.semaphore_wait(credit_x, 1)

        for a in range(len(trains)):

            @pl.when((n >= a * steps) & (n < (a + 1) * steps))
            def _():
                first_copy(trains[a], n - a * steps, slot).start()
                load_copy(trains[a], n - a * steps, slot).start()

    def stage_send(n):
        slot = lax.rem(n, buffers)
        load_copy(t0, 0, slot).wait()
        first_copy(t0, 0, slot).wait()

        @pl.when(has_up)
        def _():
            @pl.when(n >= buffers)
            def _():
                pl.semaphore_wait(credit_up, 1)

            up_copy(slot, z).start()

        @pl.when(has_down)
        def _():
            @pl.when(n >= buffers)
            def _():
                pl.semaphore_wait(credit_down, 1)

            down_copy(slot, z).start()

    def stage_forward(n, distance):
        slot = lax.rem(n, buffers)

        @pl.when(z - distance >= 0)
        def _():
            up_copy(slot, z - distance).wait_recv()

            @pl.when(has_up)
            def _():
                up_copy(slot, z - distance).start()

        @pl.when(z + distance < pairs)
        def _():
            down_copy(slot, z + distance).wait_recv()

            @pl.when(has_down)
            def _():
                down_copy(slot, z + distance).start()

    def stage_finish(n):
        slot = lax.rem(n, buffers)
        stage = lax.rem(n, 2)
        taken = pltpu.make_async_copy(held.at[slot], whole, stage_sem)
        taken.start()

        def drain_up(level, carry):
            up_copy(slot, level).wait_send()
            return carry

        def drain_down(level, carry):
            down_copy(slot, level).wait_send()
            return carry

        @pl.when(has_up)
        def _():
            lax.fori_loop(0, z + 1, drain_up, 0)

        @pl.when(has_down)
        def _():
            lax.fori_loop(z, pairs, drain_down, 0)

        taken.wait()

        @pl.when(n < total - buffers)
        def _():
            pl.semaphore_signal(credit_x, inc=1, device_id={"ep": partner}, device_id_type=MESH)

            @pl.when(has_up)
            def _():
                pl.semaphore_signal(
                    credit_down, inc=1, device_id={"ep": above}, device_id_type=MESH
                )

            @pl.when(has_down)
            def _():
                pl.semaphore_signal(
                    credit_up, inc=1, device_id={"ep": below}, device_id_type=MESH
                )

        @pl.when(n >= 2)
        def _():
            own_copy(o0, 0, stage).wait()
            other_copy(o0, 0, stage, 0).wait_send()

        @pl.when(n >= 1)
        def _():
            other_copy(o0, 0, stage, lax.rem(n - 1, recv_slots)).wait_recv()

        def pick(s, carry):
            other[stage, s] = whole[idx_ref[picks + s]]
            own[stage, s] = whole[idx_ref[s]]
            return carry

        lax.fori_loop(0, picks, pick, 0)
        for a in range(len(trains)):

            @pl.when((n >= a * steps) & (n < (a + 1) * steps))
            def _():
                other_copy(outs[a], n - a * steps, stage, lax.rem(n, recv_slots)).start()
                own_copy(outs[a], n - a * steps, stage).start()

    def iteration(i, carry):
        @pl.when(i < total)
        def _():
            stage_start(i)

        @pl.when((i >= 1) & (i - 1 < total))
        def _():
            stage_send(i - 1)

        def hop(distance, inner):
            n = i - 1 - distance

            @pl.when((n >= 0) & (n < total))
            def _():
                stage_forward(n, distance)

            return inner

        lax.fori_loop(1, pairs, hop, 0)

        @pl.when(i >= pairs)
        def _():
            stage_finish(i - pairs)

        return carry

    lax.fori_loop(0, total + pairs, iteration, 0)
    for n in range(max(total - 2, 0), total):
        own_copy(o0, 0, n % 2).wait()
        other_copy(o0, 0, n % 2, 0).wait_send()
    other_copy(o0, 0, 0, (total - 1) % recv_slots).wait_recv()


def relay(idx, trains, ep_count, part_count):
    local, piece_rows, width = trains[0].shape
    pairs = ep_count // 2
    slots = ep_count * local
    buffers = pairs + 3
    chunk_rows = 32
    while chunk_rows > 16 and buffers * slots * chunk_rows * width * 2 > 24 * 2**20:
        chunk_rows //= 2
    picks = local * part_count
    dma = pltpu.SemaphoreType.DMA
    any_spec = pl.BlockSpec(memory_space=pl.ANY)
    return pl.pallas_call(
        functools.partial(relay_kernel, pairs, chunk_rows, buffers),
        out_shape=[jax.ShapeDtypeStruct((picks, piece_rows, width), jnp.bfloat16)] * 3,
        in_specs=[pl.BlockSpec(memory_space=pltpu.SMEM)] + [any_spec] * 3,
        out_specs=[any_spec] * 3,
        scratch_shapes=[
            pltpu.VMEM((buffers, slots, chunk_rows, width), jnp.bfloat16),
            pltpu.VMEM((slots, chunk_rows, width), jnp.bfloat16),
            pltpu.VMEM((2, picks, chunk_rows, width), jnp.bfloat16),
            pltpu.VMEM((2, picks, chunk_rows, width), jnp.bfloat16),
            dma((buffers,)),
            dma((buffers,)),
            dma((buffers,)),
            dma((buffers, pairs + 1)),
            dma((buffers, pairs)),
            dma((2,)),
            dma((2,)),
            dma((buffers + 2,)),
            dma,
            pltpu.SemaphoreType.REGULAR,
            pltpu.SemaphoreType.REGULAR,
            pltpu.SemaphoreType.REGULAR,
        ],
        compiler_params=pltpu.CompilerParams(
            collective_id=0, has_side_effects=True, vmem_limit_bytes=56 * 2**20
        ),
    )(idx, *trains)


def body(
    tokens, route_ids, route_weights, train_map, serve_place, train_gate, train_up, train_down
):
    ep_count = lax.axis_size("ep")
    tp_count = lax.axis_size("tp")
    ep_index = lax.axis_index("ep")
    slot_count = serve_place.shape[0]
    local_slots, piece_rows, quarter_width = train_gate.shape
    part_count = slot_count // EXPERTS
    slot_iota = jnp.arange(slot_count, dtype=jnp.int32)
    inverse = jnp.sum(
        jnp.where(train_map[:, None] == slot_iota[None, :], slot_iota[:, None], 0), axis=0
    )
    wanted = (
        serve_place[:, None] * part_count + jnp.arange(part_count, dtype=jnp.int32)[None, :]
    ).reshape(-1)
    source_slot = jnp.sum(
        jnp.where(wanted[:, None] == slot_iota[None, :], inverse[None, :], 0), axis=1
    ).reshape(ep_count, local_slots * part_count)
    partner = ep_index + 1 - 2 * (ep_index % 2)
    idx = jnp.concatenate(
        [
            lax.dynamic_index_in_dim(source_slot, ep_index, 0, keepdims=False),
            lax.dynamic_index_in_dim(source_slot, partner, 0, keepdims=False),
        ]
    ).astype(jnp.int32)
    model_rows = part_count * piece_rows
    raw_gate, raw_up, raw_down = (
        o.reshape(local_slots, model_rows, quarter_width)
        for o in relay(idx, (train_gate, train_up, train_down), ep_count, part_count)
    )

    step_count, tok_count, model_width = tokens.shape
    topk_count = route_ids.shape[2]
    capacity = (MOST + 1) // 2
    depth = capacity * step_count
    peer_rows = depth * local_slots
    all_tokens = step_count * tok_count
    same_slot = serve_place[:, None] == serve_place[None, :]
    replica_rank = jnp.sum(same_slot & (slot_iota[None, :] < slot_iota[:, None]), axis=1)
    pair_count = tok_count * topk_count
    pair_iota = jnp.arange(pair_count, dtype=jnp.int32)

    def rows(ids, decode_step):
        pair_experts = ids.reshape(pair_count)
        holders = serve_place[None, :] == pair_experts[:, None]
        replica_count = jnp.sum(holders, axis=1)
        earlier_pairs = (pair_experts[:, None] == pair_experts[None, :]) & (
            pair_iota[None, :] < pair_iota[:, None]
        )
        seen = jnp.sum(earlier_pairs, axis=1)
        target = (seen + ep_index) % replica_count
        position = seen // replica_count
        chosen = holders & (replica_rank[None, :] == target[:, None])
        dest_slot = jnp.sum(jnp.where(chosen, slot_iota[None, :], 0), axis=1)
        return (
            dest_slot // local_slots * peer_rows
            + (decode_step * capacity + position) * local_slots
            + dest_slot % local_slots
        )

    row_index = jax.vmap(rows)(route_ids, jnp.arange(step_count, dtype=jnp.int32))
    row_index = row_index.reshape(1, all_tokens, topk_count)
    buffer_iota = jnp.arange(ep_count * peer_rows, dtype=jnp.int32)
    placing = row_index == buffer_iota[:, None, None]
    mixing = jnp.sum(
        jnp.where(placing, route_weights.reshape(1, all_tokens, topk_count), 0.0), axis=2
    )
    send_rows = jnp.dot(
        jnp.any(placing, axis=2).astype(jnp.bfloat16),
        tokens.reshape(all_tokens, model_width),
        preferred_element_type=jnp.float32,
    ).astype(jnp.bfloat16)
    received = lax.all_to_all(
        send_rows.reshape(ep_count, depth, local_slots, model_width),
        "ep", split_axis=0, concat_axis=0, tiled=True,
    ).reshape(ep_count * depth, local_slots, model_width)
    mix = lax.all_to_all(
        mixing.reshape(ep_count, peer_rows, all_tokens),
        "ep", split_axis=0, concat_axis=0, tiled=True,
    )
    gate_act = jnp.einsum("mld,ldf->lmf", received, raw_gate, preferred_element_type=jnp.float32)
    up_act = jnp.einsum("mld,ldf->lmf", received, raw_up, preferred_element_type=jnp.float32)
    hidden = (jax.nn.silu(gate_act) * up_act).astype(jnp.bfloat16)
    partial_value = jnp.einsum(
        "lmf,ldf->lmd", hidden, raw_down, preferred_element_type=jnp.float32
    ).astype(jnp.bfloat16)
    mix = mix.reshape(ep_count, depth, local_slots, all_tokens)
    mix_high = mix.astype(jnp.bfloat16)
    mix_low = (mix - mix_high.astype(jnp.float32)).astype(jnp.bfloat16)
    rows_out = partial_value.reshape(local_slots, ep_count, depth, model_width)

    def combine(part):
        return jnp.einsum("pclt,lpcd->ptd", part, rows_out, preferred_element_type=jnp.float32)

    combined = (combine(mix_high) + combine(mix_low)).astype(jnp.bfloat16)
    combined = lax.optimization_barrier(combined)
    summed = lax.psum_scatter(combined, "tp", scatter_dimension=2, tiled=True)
    raw_gate, raw_up, raw_down, _ = lax.optimization_barrier(
        (raw_gate, raw_up, raw_down, combined)
    )
    serve_gate, serve_up, serve_down = (settle(o) for o in (raw_gate, raw_up, raw_down))
    summed, serve_gate, serve_up = lax.optimization_barrier((summed, serve_gate, serve_up))
    returned = lax.all_to_all(summed, "ep", split_axis=0, concat_axis=0, tiled=True)
    moe_out = jnp.sum(returned.astype(jnp.float32), axis=0).astype(jnp.bfloat16)
    moe_out = moe_out.reshape(step_count, tok_count, model_width // tp_count)
    return (serve_gate, serve_up, serve_down, moe_out)


def stream_kernel(
    levels, cap, cap_x, buffers, idx_ref, tok_ref, mix_ref, t0, t1, t2, o0, o1, o2, part_ref,
    firsts, lows, highs, crosses, ups, downs, across, stage, tokens, mix, acc, hid, flipped,
    load_sem, first_send, first_recv, up_send, up_recv, down_send, down_recv,
    across_send, cross_recv, cross_load, out_sem, tok_send, tok_recv, mix_send, mix_recv,
    here_sem, credit_first, credit_up, credit_down, credit_cross,
):
    trains, outs = (t0, t1, t2), (o0, o1, o2)
    me = lax.axis_index("ep")
    ep_count = 2 * levels
    z, x = lax.div(me, 2), lax.rem(me, 2)
    partner = me + 1 - 2 * x
    above, below = me + 2, me - 2
    local, _, half, width = t0.shape
    layer = 2 * local
    chunk = ups.shape[2]
    steps = half // chunk
    total = len(trains) * steps
    parts = stage.shape[1] // local
    depth = parts * 2 * chunk
    cross_slots = len(crosses)
    first_slots = firsts.shape[0]
    stages = stage.shape[0]
    group = depth // chunk
    tok_rows = tok_ref.shape[0]
    up_at, down_at = 0, UP_ROOM
    cross_at = 2 * UP_ROOM
    own_at = cross_at + parts * local
    other_at = own_at + parts * local
    high_at = 3 * parts * local
    has_up, has_down = z < levels - 1, z > 0

    def to(device):
        return {"device_id": {"ep": device}, "device_id_type": MESH}

    barrier = pltpu.get_barrier_semaphore()

    def greet(k, carry):
        pl.semaphore_signal(barrier, inc=1, **to(lax.rem(me + k, ep_count)))
        return carry

    lax.fori_loop(1, ep_count, greet, 0)
    pl.semaphore_wait(barrier, ep_count - 1)

    def rows_of(step):
        return pl.ds(pl.multiple_of(step * chunk, chunk), chunk)

    def tok_copy(k):
        return pltpu.make_async_remote_copy(
            src_ref=tok_ref,
            dst_ref=tokens.at[pl.ds(pl.multiple_of(me * tok_rows, 16), tok_rows)],
            send_sem=tok_send.at[k],
            recv_sem=tok_recv.at[k],
            **to(lax.rem(me + k, ep_count)),
        )

    def mix_copy(k):
        peer = lax.rem(me + k, ep_count)
        return pltpu.make_async_remote_copy(
            src_ref=mix_ref.at[peer],
            dst_ref=mix.at[pl.ds(pl.multiple_of(me * tok_rows, 16), tok_rows)],
            send_sem=mix_send.at[k],
            recv_sem=mix_recv.at[k],
            **to(peer),
        )

    def tok_here():
        return pltpu.make_async_copy(
            tok_ref, tokens.at[pl.ds(pl.multiple_of(me * tok_rows, 16), tok_rows)], here_sem.at[0]
        )

    def mix_here():
        return pltpu.make_async_copy(
            mix_ref.at[me], mix.at[pl.ds(pl.multiple_of(me * tok_rows, 16), tok_rows)],
            here_sem.at[1],
        )

    def load_copy(train, step, slot):
        return pltpu.make_async_copy(
            train.at[:, x, rows_of(step), :],
            firsts.at[slot, pl.ds(x * local, local)],
            load_sem.at[slot],
        )

    def first_copy(train, step, slot):
        return pltpu.make_async_remote_copy(
            src_ref=train.at[:, 1 - x, rows_of(step), :],
            dst_ref=firsts.at[slot, pl.ds(x * local, local)],
            send_sem=first_send.at[slot],
            recv_sem=first_recv.at[slot],
            **to(partner),
        )

    def own_cross_copy(train, step, slot):
        return pltpu.make_async_copy(
            train.at[:, 1 - x, rows_of(step), :], crosses[slot].at[pl.ds(0, local)],
            cross_load.at[slot],
        )

    def up_copy(side, slot):
        return pltpu.make_async_remote_copy(
            src_ref=ups.at[side],
            dst_ref=lows[slot].at[pl.ds(layer, cap)],
            send_sem=up_send.at[side],
            recv_sem=up_recv.at[slot],
            **to(above),
        )

    def down_copy(side, slot):
        return pltpu.make_async_remote_copy(
            src_ref=downs.at[side],
            dst_ref=highs[slot].at[pl.ds(layer, cap)],
            send_sem=down_send.at[side],
            recv_sem=down_recv.at[slot],
            **to(below),
        )

    def across_copy(side, slot):
        return pltpu.make_async_remote_copy(
            src_ref=across.at[side],
            dst_ref=crosses[slot].at[pl.ds(local, cap_x)],
            send_sem=across_send.at[side],
            recv_sem=cross_recv.at[slot],
            **to(partner),
        )

    def out_copy(out, step, place):
        return pltpu.make_async_copy(
            stage.at[place], out.at[:, :, rows_of(step), :], out_sem.at[place]
        )

    def each_array(n, action):
        for a in range(len(trains)):

            @pl.when((n >= a * steps) & (n < (a + 1) * steps))
            def _():
                action(a, n - a * steps)

    def each_slot(n, count, action):
        for b in range(count):

            @pl.when(lax.rem(n, count) == b)
            def _():
                action(b)

    def gather(count, put, take):
        wide = 4

        def several(g, carry):
            for k in range(wide):
                put(g * wide + k, take(g * wide + k))
            return carry

        lax.fori_loop(0, count // wide, several, 0)
        for j in range(count // wide * wide, count):
            put(j, take(j))

    def start(n):
        slot = lax.rem(n, first_slots)

        @pl.when(n >= first_slots)
        def _():
            pl.semaphore_wait(credit_first, 1)

        def go(a, step):
            first_copy(trains[a], step, slot).start()
            load_copy(trains[a], step, slot).start()

        each_array(n, go)

    def settle_first(n):
        place = lax.rem(n, first_slots)
        load_copy(t0, 0, place).wait()
        first_copy(t0, 0, place).wait()

        def go(slot):
            def both(j, value):
                lows[slot][j] = value
                highs[slot][j] = value

            gather(layer, both, lambda j: firsts[place, j])

        each_slot(n, buffers, go)

        @pl.when(n < total - first_slots)
        def _():
            pl.semaphore_signal(credit_first, inc=1, **to(partner))

    def send_up(n):
        side = lax.rem(n, 2)

        @pl.when(has_up & (n >= 2))
        def _():
            up_copy(side, 0).wait_send()

        def put(j, value):
            ups[side, j] = value

        def go(slot):
            @pl.when(has_down)
            def _():
                up_copy(side, slot).wait_recv()

            @pl.when(has_up)
            def _():
                gather(cap, put, lambda j: lows[slot][idx_ref[up_at + j]])

                @pl.when(n >= buffers)
                def _():
                    pl.semaphore_wait(credit_up, 1)

                up_copy(side, slot).start()

        each_slot(n, buffers, go)

    def send_down(n):
        side = lax.rem(n, 2)

        @pl.when(has_down & (n >= 2))
        def _():
            down_copy(side, 0).wait_send()

        def put(j, value):
            downs[side, j] = value

        def go(slot):
            @pl.when(has_up)
            def _():
                down_copy(side, slot).wait_recv()

            @pl.when(has_down)
            def _():
                gather(cap, put, lambda j: highs[slot][idx_ref[down_at + j]])

                @pl.when(n >= buffers)
                def _():
                    pl.semaphore_wait(credit_down, 1)

                down_copy(side, slot).start()

        each_slot(n, buffers, go)

    def send_across(n):
        side = lax.rem(n, 2)
        place = lax.rem(n, stages)

        @pl.when(n >= 2)
        def _():
            across_copy(side, 0).wait_send()

        def put(j, value):
            across[side, j] = value

        def either(slot, j):
            high = idx_ref[j + high_at]
            return jnp.where(high > 0, highs[slot][high], lows[slot][idx_ref[j]])

        def pack(slot):
            gather(cap_x, put, lambda j: either(slot, cross_at + j))

        each_slot(n, buffers, pack)

        @pl.when(n >= cross_slots)
        def _():
            pl.semaphore_wait(credit_cross, 1)

        each_slot(n, cross_slots, lambda b: across_copy(side, b).start())

        @pl.when(n >= stages)
        def _():
            out_copy(o0, 0, place).wait()

        def keep(j, value):
            stage[place, j, x] = value

        def own(slot):
            gather(parts * local, keep, lambda j: either(slot, own_at + j))

        each_slot(n, buffers, own)

        @pl.when(n < total - buffers)
        def _():
            @pl.when(has_up)
            def _():
                pl.semaphore_signal(credit_down, inc=1, **to(above))

            @pl.when(has_down)
            def _():
                pl.semaphore_signal(credit_up, inc=1, **to(below))

    def load_cross(n):
        def go(slot, a, step):
            own_cross_copy(trains[a], step, slot).start()

        each_slot(n, cross_slots, lambda b: each_array(n, functools.partial(go, b)))

    def slot_weights(place, s):
        rows = stage[place, pl.ds(s * parts, parts)]
        return rows.reshape(depth, width)

    def finish(n):
        place = lax.rem(n, stages)
        step = lax.rem(n, steps)

        def keep(j, value):
            stage[place, j, 1 - x] = value

        def other(slot):
            across_copy(0, slot).wait_recv()
            own_cross_copy(t0, 0, slot).wait()
            gather(parts * local, keep, lambda j: crosses[slot][idx_ref[other_at + j]])

        each_slot(n, cross_slots, other)
        each_array(n, lambda a, at: out_copy(outs[a], at, place).start())

        @pl.when(n < total - cross_slots)
        def _():
            pl.semaphore_signal(credit_cross, inc=1, **to(partner))

        @pl.when(n == 0)
        def _():
            tok_here().wait()
            mix_here().wait()

            def arrive(k, carry):
                tok_copy(k).wait()
                mix_copy(k).wait()
                return carry

            lax.fori_loop(1, ep_count, arrive, 0)

        @pl.when(n < 2 * steps)
        def _():
            which = lax.div(n, steps)
            lhs = tokens[:, pl.ds(pl.multiple_of(step * depth, depth), depth)]

            def add(s, carry):
                acc[which, s] += jnp.dot(
                    lhs, slot_weights(place, s), preferred_element_type=jnp.float32
                )
                return carry

            lax.fori_loop(0, local, add, 0)

        @pl.when(n == 2 * steps)
        def _():
            block = 128
            lane = lax.broadcasted_iota(jnp.int32, (block, mix.shape[1]), 1)

            def act(i, carry):
                s, b = lax.div(i, tokens.shape[0] // block), lax.rem(i, tokens.shape[0] // block)
                span = pl.ds(pl.multiple_of(b * block, block), block)
                scale = jnp.sum(jnp.where(lane == s, mix[span, :], 0.0), axis=1, keepdims=True)
                gate = acc[0, s, span, :]
                value = gate / (1.0 + jnp.exp(-gate)) * acc[1, s, span, :] * scale
                hid[s, :, span] = value.T.astype(jnp.bfloat16)
                return carry

            lax.fori_loop(0, local * (tokens.shape[0] // block), act, 0)

        @pl.when(n >= 2 * steps)
        def _():
            def add(s, carry):
                return carry + jnp.dot(
                    slot_weights(place, s), hid[s], preferred_element_type=jnp.float32
                )

            mixed = lax.fori_loop(
                0, local, add, jnp.zeros((depth, tokens.shape[0]), jnp.float32)
            )
            inner = lax.rem(step, group)
            for k in range(2 * parts):
                flipped[k, pl.ds(pl.multiple_of(inner * chunk, chunk), chunk), :] = mixed[
                    k * chunk : (k + 1) * chunk
                ]

            @pl.when(inner == group - 1)
            def _():
                for k in range(2 * parts):
                    at = k * half + lax.div(step, group) * depth
                    part_ref[:, pl.ds(pl.multiple_of(at, depth), depth)] = flipped[k].T.astype(
                        jnp.bfloat16
                    )

    def spread(k, carry):
        tok_copy(k).start()
        mix_copy(k).start()
        return carry

    lax.fori_loop(1, ep_count, spread, 0)
    tok_here().start()
    mix_here().start()

    def clear(s, carry):
        for a in range(2):
            acc[a, s] = jnp.zeros(acc.shape[2:], jnp.float32)
        return carry

    def within(n):
        return (n >= 0) & (n < total)

    def iteration(i, carry):
        @pl.when(i < total)
        def _():
            start(i)

        @pl.when(within(i - 1))
        def _():
            settle_first(i - 1)

        n_up = i - 1 - z

        @pl.when(within(n_up))
        def _():
            send_up(n_up)

        n_down = i - levels + z

        @pl.when(within(n_down))
        def _():
            send_down(n_down)

        @pl.when(within(i - levels + 1))
        def _():
            load_cross(i - levels + 1)

        @pl.when(within(i - levels))
        def _():
            send_across(i - levels)

        @pl.when(i == 0)
        def _():
            lax.fori_loop(0, local, clear, 0)

        @pl.when(within(i - levels - 1))
        def _():
            finish(i - levels - 1)

        return carry

    lax.fori_loop(0, total + levels + 1, iteration, 0)
    for n in range(total - 2, total):

        @pl.when(has_up)
        def _():
            up_copy(n % 2, 0).wait_send()

        @pl.when(has_down)
        def _():
            down_copy(n % 2, 0).wait_send()

        across_copy(n % 2, 0).wait_send()
    for n in range(total - stages, total):
        out_copy(o0, 0, n % stages).wait()


def stream(idx, tok, mix, trains, ep_count, part_count, cap, collective):
    local, _, half, width = trains[0].shape
    levels = ep_count // 2
    chunk = 16
    buffers = levels + 3
    cross_slots = 4
    stages = 3
    picks = local * part_count
    cap_x = min(cap - local, picks)
    all_tokens = ep_count * tok.shape[0]
    depth = 2 * part_count * chunk
    dma = pltpu.SemaphoreType.DMA
    any_spec = pl.BlockSpec(memory_space=pl.ANY)
    bf16, f32 = jnp.bfloat16, jnp.float32
    return pl.pallas_call(
        functools.partial(stream_kernel, levels, cap, cap_x, buffers),
        out_shape=[jax.ShapeDtypeStruct((picks, 2, half, width), bf16)] * 3
        + [jax.ShapeDtypeStruct((all_tokens, tok.shape[1]), bf16)],
        in_specs=[pl.BlockSpec(memory_space=pltpu.SMEM)] + [any_spec] * 5,
        out_specs=[any_spec] * 3 + [pl.BlockSpec(memory_space=pltpu.VMEM)],
        scratch_shapes=[
            pltpu.VMEM((4, 2 * local, chunk, width), bf16),
            [pltpu.VMEM((2 * local + cap, chunk, width), bf16)] * buffers,
            [pltpu.VMEM((2 * local + cap, chunk, width), bf16)] * buffers,
            [pltpu.VMEM((local + cap_x, chunk, width), bf16)] * cross_slots,
            pltpu.VMEM((2, cap, chunk, width), bf16),
            pltpu.VMEM((2, cap, chunk, width), bf16),
            pltpu.VMEM((2, cap_x, chunk, width), bf16),
            pltpu.VMEM((stages, picks, 2, chunk, width), bf16),
            pltpu.VMEM((all_tokens, tok.shape[1]), bf16),
            pltpu.VMEM((all_tokens, mix.shape[2]), f32),
            pltpu.VMEM((2, local, all_tokens, width), f32),
            pltpu.VMEM((local, width, all_tokens), bf16),
            pltpu.VMEM((2 * part_count, depth, all_tokens), f32),
            dma((4,)),
            dma((4,)),
            dma((4,)),
            dma((2,)),
            dma((buffers,)),
            dma((2,)),
            dma((buffers,)),
            dma((2,)),
            dma((cross_slots,)),
            dma((cross_slots,)),
            dma((stages,)),
            dma((ep_count,)),
            dma((ep_count,)),
            dma((ep_count,)),
            dma((ep_count,)),
            dma((2,)),
            pltpu.SemaphoreType.REGULAR,
            pltpu.SemaphoreType.REGULAR,
            pltpu.SemaphoreType.REGULAR,
            pltpu.SemaphoreType.REGULAR,
        ],
        compiler_params=pltpu.CompilerParams(
            collective_id=collective, has_side_effects=True, vmem_limit_bytes=56 * 2**20
        ),
    )(idx, tok, mix, *trains)


def routing(train_map, serve_place, ep_index, ep_count, local, parts):
    slots = train_map.shape[0]
    levels = ep_count // 2
    layer = 2 * local
    held = jnp.arange(slots, dtype=jnp.int32)
    level, owner = held // layer, held // local
    devices = jnp.arange(ep_count, dtype=jnp.int32)
    floors = jnp.arange(levels, dtype=jnp.int32)
    wanted = serve_place.reshape(ep_count, local)
    need = jnp.any(wanted[:, :, None] == (train_map // parts)[None, None, :], axis=1)
    need_level = jnp.any(need.reshape(levels, 2, slots), axis=1)
    higher = floors[None, :, None] > floors[:, None, None]
    lower = floors[None, :, None] < floors[:, None, None]
    up = jnp.any(higher & need_level[None], axis=1) & (level[None, :] <= floors[:, None])
    down = jnp.any(lower & need_level[None], axis=1) & (level[None, :] >= floors[:, None])
    partner_need = need.reshape(levels, 2, slots)[:, ::-1].reshape(ep_count, slots)
    partners = devices + 1 - 2 * (devices % 2)
    cross = partner_need & (owner[None, :] != partners[:, None])
    flags = jnp.concatenate([up, down, cross], axis=0)
    before = (held[:, None] < held[None, :]).astype(jnp.bfloat16)
    place = jnp.dot(
        flags.astype(jnp.bfloat16), before, preferred_element_type=jnp.float32
    ).astype(jnp.int32)
    counts = jnp.sum(flags.astype(jnp.int32), axis=1)
    needed = jnp.maximum(
        jnp.max(counts[: 2 * levels]), jnp.max(counts[2 * levels :]) + local
    )

    def tables():
        z = ep_index // 2
        partner = ep_index + 1 - 2 * (ep_index % 2)

        def row(array, at):
            return lax.dynamic_index_in_dim(array, at, 0, keepdims=False)

        from_below = row(place, jnp.maximum(z - 1, 0))
        from_above = row(place, levels + jnp.minimum(z + 1, levels - 1))
        from_partner = row(place, 2 * levels + partner)
        here = held - layer * z
        where_low = jnp.where(level == z, here, jnp.where(level < z, layer + from_below, 0))
        where_high = jnp.where(level > z, layer + from_above, 0)
        where_cross = jnp.where(owner == ep_index, held - local * ep_index, local + from_partner)

        def listed(at, room, where):
            hit = row(flags, at)[None, :] & (
                row(place, at)[None, :] == jnp.arange(room, dtype=jnp.int32)[:, None]
            )
            return jnp.sum(jnp.where(hit, where[None, :], 0), axis=1)

        mine = (
            row(wanted, ep_index)[:, None] * parts + jnp.arange(parts, dtype=jnp.int32)[None, :]
        ).reshape(-1)
        same = mine[:, None] == train_map[None, :]
        def picked(where):
            return jnp.sum(jnp.where(same, where[None, :], 0), axis=1)

        room, at = parts * local, 2 * levels + ep_index
        return jnp.concatenate(
            [
                listed(z, UP_ROOM, where_low),
                listed(levels + z, UP_ROOM, where_high + jnp.where(level == z, here, 0)),
                listed(at, room, where_low),
                picked(where_low),
                picked(where_cross),
                listed(at, room, where_high),
                picked(where_high),
            ]
        ).astype(jnp.int32)

    return needed, tables


def stream_body(
    tokens, route_ids, route_weights, train_map, serve_place, train_gate, train_up, train_down
):
    ep_count = lax.axis_size("ep")
    tp_count = lax.axis_size("tp")
    ep_index = lax.axis_index("ep")
    slot_count = serve_place.shape[0]
    local, piece_rows, width = train_gate.shape
    parts = slot_count // EXPERTS
    step_count, tok_count, model_width = tokens.shape
    topk_count = route_ids.shape[2]
    rows = step_count * tok_count
    half, chunk = piece_rows // 2, 16
    full = slot_count - 2 * local
    caps = [c for c in CAPS if c < full] + [full]

    slot_iota = jnp.arange(slot_count, dtype=jnp.int32)
    first = ~jnp.any(
        (serve_place[:, None] == serve_place[None, :]) & (slot_iota[None, :] < slot_iota[:, None]),
        axis=1,
    )
    holder = jnp.where(first, serve_place, -1)
    ids = route_ids.reshape(rows, topk_count)
    weights = route_weights.reshape(rows, topk_count)
    mix = jnp.sum(
        jnp.where(ids[:, :, None] == holder[None, None, :], weights[:, :, None], 0.0), axis=1
    )
    mix = mix.reshape(rows, ep_count, local).transpose(1, 0, 2)
    mix = jnp.pad(mix, ((0, 0), (0, 0), (0, 128 - local)))
    ordered = (
        tokens.reshape(rows, 2 * parts, half // chunk, chunk)
        .transpose(0, 2, 1, 3)
        .reshape(rows, model_width)
    )
    needed, tables = routing(train_map, serve_place, ep_index, ep_count, local, parts)
    choice = sum((needed > c).astype(jnp.int32) for c in caps[:-1])
    idx = tables()
    trains = [t.reshape(local, 2, half, width) for t in (train_gate, train_up, train_down)]

    def run(collective, cap_static):
        def branch(idx, ordered, mix, *trains):
            return tuple(
                stream(idx, ordered, mix, trains, ep_count, parts, cap_static, collective)
            )

        return branch

    raw_gate, raw_up, raw_down, combined = lax.switch(
        choice, [run(k, c) for k, c in enumerate(caps)], idx, ordered, mix, *trains
    )
    raw_gate, raw_up, raw_down = (
        o.reshape(local, model_width, width) for o in (raw_gate, raw_up, raw_down)
    )
    combined = combined.reshape(ep_count, rows, model_width)
    summed = lax.psum_scatter(combined, "tp", scatter_dimension=2, tiled=True)
    serve_gate, serve_up, serve_down = (settle(o) for o in (raw_gate, raw_up, raw_down))
    summed, serve_gate, serve_up = lax.optimization_barrier((summed, serve_gate, serve_up))
    returned = lax.all_to_all(summed, "ep", split_axis=0, concat_axis=0, tiled=True)
    moe_out = jnp.sum(returned.astype(jnp.float32), axis=0).astype(jnp.bfloat16)
    moe_out = moe_out.reshape(step_count, tok_count, model_width // tp_count)
    return (serve_gate, serve_up, serve_down, moe_out)


def settle_kernel(source, target):
    target[...] = source[...]


def settle(source):
    slots, rows, width = source.shape
    spec = pl.BlockSpec((1, rows, width), lambda i: (i, 0, 0))
    return pl.pallas_call(
        settle_kernel,
        grid=(slots,),
        out_shape=jax.ShapeDtypeStruct(source.shape, source.dtype),
        in_specs=[spec],
        out_specs=spec,
        cost_estimate=pl.CostEstimate(
            flops=0, bytes_accessed=4 * slots * rows * width, transcendentals=0
        ),
    )(source)


def solution(mesh):
    in_specs = (
        P(None, "ep", None),
        P(None, "ep", None),
        P(None, "ep", None),
        P(),
        P(),
        P("ep", None, "tp"),
        P("ep", None, "tp"),
        P("ep", None, "tp"),
    )
    out_specs = (P("ep", None, "tp"), P("ep", None, "tp"), P("ep", None, "tp"), P(None, "ep", "tp"))
    chosen = stream_body if mesh.shape["ep"] <= 8 else body
    return jax.shard_map(chosen, mesh=mesh, in_specs=in_specs, out_specs=out_specs, check_vma=False)
```

```python
import functools

import jax
import jax.numpy as jnp
from jax import lax
from jax.experimental import pallas as pl
from jax.experimental.pallas import tpu as pltpu
from jax.sharding import PartitionSpec as P

EXPERTS = 16
MOST = 10
MESH = pl.DeviceIdType.MESH
CAPS = (32, 33, 34, 35, 36, 37, 38, 40)
UP_ROOM = 48


def relay_kernel(
    pairs, chunk_rows, buffers, idx_ref, t0, t1, t2, o0, o1, o2, held, whole, own, other,
    local_sem, first_send, first_recv, line_send, line_recv,
    own_sem, other_send, other_recv, stage_sem, credit_x, credit_up, credit_down,
):
    trains, outs = (t0, t1, t2), (o0, o1, o2)
    me = lax.axis_index("ep")
    z, x = lax.div(me, 2), lax.rem(me, 2)
    partner = me + 1 - 2 * x
    above, below = me + 2, me - 2
    local = t0.shape[0]
    half = t0.shape[1] // 2
    steps = half // chunk_rows
    total = len(trains) * steps
    layer = 2 * local
    picks = own.shape[1]
    recv_slots = other_recv.shape[0]
    has_up, has_down = z < pairs - 1, z > 0

    barrier = pltpu.get_barrier_semaphore()
    pl.semaphore_signal(barrier, inc=1, device_id={"ep": partner}, device_id_type=MESH)

    @pl.when(has_up)
    def _():
        pl.semaphore_signal(barrier, inc=1, device_id={"ep": above}, device_id_type=MESH)

    @pl.when(has_down)
    def _():
        pl.semaphore_signal(barrier, inc=1, device_id={"ep": below}, device_id_type=MESH)

    pl.semaphore_wait(barrier, 1 + jnp.where(has_up, 1, 0) + jnp.where(has_down, 1, 0))

    def rows_of(side, step):
        return pl.ds(pl.multiple_of(side * half + step * chunk_rows, chunk_rows), chunk_rows)

    def mine(slot):
        return held.at[slot, pl.ds(me * local, local)]

    def region(slot, level):
        return held.at[slot, pl.ds(level * layer, layer)]

    def load_copy(train, step, slot):
        return pltpu.make_async_copy(
            train.at[:, rows_of(x, step), :], mine(slot), local_sem.at[slot]
        )

    def first_copy(train, step, slot):
        return pltpu.make_async_remote_copy(
            src_ref=train.at[:, rows_of(1 - x, step), :],
            dst_ref=mine(slot),
            send_sem=first_send.at[slot],
            recv_sem=first_recv.at[slot],
            device_id={"ep": partner},
            device_id_type=MESH,
        )

    def up_copy(slot, level):
        return pltpu.make_async_remote_copy(
            src_ref=region(slot, level),
            dst_ref=region(slot, level),
            send_sem=line_send.at[slot, level],
            recv_sem=line_recv.at[slot, level],
            device_id={"ep": above},
            device_id_type=MESH,
        )

    def down_copy(slot, level):
        return pltpu.make_async_remote_copy(
            src_ref=region(slot, level),
            dst_ref=region(slot, level),
            send_sem=line_send.at[slot, level + 1],
            recv_sem=line_recv.at[slot, level],
            device_id={"ep": below},
            device_id_type=MESH,
        )

    def own_copy(out, step, stage):
        return pltpu.make_async_copy(
            own.at[stage], out.at[:, rows_of(x, step), :], own_sem.at[stage]
        )

    def other_copy(out, step, stage, recv_slot):
        return pltpu.make_async_remote_copy(
            src_ref=other.at[stage],
            dst_ref=out.at[:, rows_of(x, step), :],
            send_sem=other_send.at[stage],
            recv_sem=other_recv.at[recv_slot],
            device_id={"ep": partner},
            device_id_type=MESH,
        )

    def stage_start(n):
        slot = lax.rem(n, buffers)

        @pl.when(n >= buffers)
        def _():
            pl.semaphore_wait(credit_x, 1)

        for a in range(len(trains)):

            @pl.when((n >= a * steps) & (n < (a + 1) * steps))
            def _():
                first_copy(trains[a], n - a * steps, slot).start()
                load_copy(trains[a], n - a * steps, slot).start()

    def stage_send(n):
        slot = lax.rem(n, buffers)
        load_copy(t0, 0, slot).wait()
        first_copy(t0, 0, slot).wait()

        @pl.when(has_up)
        def _():
            @pl.when(n >= buffers)
            def _():
                pl.semaphore_wait(credit_up, 1)

            up_copy(slot, z).start()

        @pl.when(has_down)
        def _():
            @pl.when(n >= buffers)
            def _():
                pl.semaphore_wait(credit_down, 1)

            down_copy(slot, z).start()

    def stage_forward(n, distance):
        slot = lax.rem(n, buffers)

        @pl.when(z - distance >= 0)
        def _():
            up_copy(slot, z - distance).wait_recv()

            @pl.when(has_up)
            def _():
                up_copy(slot, z - distance).start()

        @pl.when(z + distance < pairs)
        def _():
            down_copy(slot, z + distance).wait_recv()

            @pl.when(has_down)
            def _():
                down_copy(slot, z + distance).start()

    def stage_finish(n):
        slot = lax.rem(n, buffers)
        stage = lax.rem(n, 2)
        taken = pltpu.make_async_copy(held.at[slot], whole, stage_sem)
        taken.start()

        def drain_up(level, carry):
            up_copy(slot, level).wait_send()
            return carry

        def drain_down(level, carry):
            down_copy(slot, level).wait_send()
            return carry

        @pl.when(has_up)
        def _():
            lax.fori_loop(0, z + 1, drain_up, 0)

        @pl.when(has_down)
        def _():
            lax.fori_loop(z, pairs, drain_down, 0)

        taken.wait()

        @pl.when(n < total - buffers)
        def _():
            pl.semaphore_signal(credit_x, inc=1, device_id={"ep": partner}, device_id_type=MESH)

            @pl.when(has_up)
            def _():
                pl.semaphore_signal(
                    credit_down, inc=1, device_id={"ep": above}, device_id_type=MESH
                )

            @pl.when(has_down)
            def _():
                pl.semaphore_signal(
                    credit_up, inc=1, device_id={"ep": below}, device_id_type=MESH
                )

        @pl.when(n >= 2)
        def _():
            own_copy(o0, 0, stage).wait()
            other_copy(o0, 0, stage, 0).wait_send()

        @pl.when(n >= 1)
        def _():
            other_copy(o0, 0, stage, lax.rem(n - 1, recv_slots)).wait_recv()

        def pick(s, carry):
            other[stage, s] = whole[idx_ref[picks + s]]
            own[stage, s] = whole[idx_ref[s]]
            return carry

        lax.fori_loop(0, picks, pick, 0)
        for a in range(len(trains)):

            @pl.when((n >= a * steps) & (n < (a + 1) * steps))
            def _():
                other_copy(outs[a], n - a * steps, stage, lax.rem(n, recv_slots)).start()
                own_copy(outs[a], n - a * steps, stage).start()

    def iteration(i, carry):
        @pl.when(i < total)
        def _():
            stage_start(i)

        @pl.when((i >= 1) & (i - 1 < total))
        def _():
            stage_send(i - 1)

        def hop(distance, inner):
            n = i - 1 - distance

            @pl.when((n >= 0) & (n < total))
            def _():
                stage_forward(n, distance)

            return inner

        lax.fori_loop(1, pairs, hop, 0)

        @pl.when(i >= pairs)
        def _():
            stage_finish(i - pairs)

        return carry

    lax.fori_loop(0, total + pairs, iteration, 0)
    for n in range(max(total - 2, 0), total):
        own_copy(o0, 0, n % 2).wait()
        other_copy(o0, 0, n % 2, 0).wait_send()
    other_copy(o0, 0, 0, (total - 1) % recv_slots).wait_recv()


def relay(idx, trains, ep_count, part_count):
    local, piece_rows, width = trains[0].shape
    pairs = ep_count // 2
    slots = ep_count * local
    buffers = pairs + 3
    chunk_rows = 32
    while chunk_rows > 16 and buffers * slots * chunk_rows * width * 2 > 24 * 2**20:
        chunk_rows //= 2
    picks = local * part_count
    dma = pltpu.SemaphoreType.DMA
    any_spec = pl.BlockSpec(memory_space=pl.ANY)
    return pl.pallas_call(
        functools.partial(relay_kernel, pairs, chunk_rows, buffers),
        out_shape=[jax.ShapeDtypeStruct((picks, piece_rows, width), jnp.bfloat16)] * 3,
        in_specs=[pl.BlockSpec(memory_space=pltpu.SMEM)] + [any_spec] * 3,
        out_specs=[any_spec] * 3,
        scratch_shapes=[
            pltpu.VMEM((buffers, slots, chunk_rows, width), jnp.bfloat16),
            pltpu.VMEM((slots, chunk_rows, width), jnp.bfloat16),
            pltpu.VMEM((2, picks, chunk_rows, width), jnp.bfloat16),
            pltpu.VMEM((2, picks, chunk_rows, width), jnp.bfloat16),
            dma((buffers,)),
            dma((buffers,)),
            dma((buffers,)),
            dma((buffers, pairs + 1)),
            dma((buffers, pairs)),
            dma((2,)),
            dma((2,)),
            dma((buffers + 2,)),
            dma,
            pltpu.SemaphoreType.REGULAR,
            pltpu.SemaphoreType.REGULAR,
            pltpu.SemaphoreType.REGULAR,
        ],
        compiler_params=pltpu.CompilerParams(
            collective_id=0, has_side_effects=True, vmem_limit_bytes=56 * 2**20
        ),
    )(idx, *trains)


def body(
    tokens, route_ids, route_weights, train_map, serve_place, train_gate, train_up, train_down
):
    ep_count = lax.axis_size("ep")
    tp_count = lax.axis_size("tp")
    ep_index = lax.axis_index("ep")
    slot_count = serve_place.shape[0]
    local_slots, piece_rows, quarter_width = train_gate.shape
    part_count = slot_count // EXPERTS
    slot_iota = jnp.arange(slot_count, dtype=jnp.int32)
    inverse = jnp.sum(
        jnp.where(train_map[:, None] == slot_iota[None, :], slot_iota[:, None], 0), axis=0
    )
    wanted = (
        serve_place[:, None] * part_count + jnp.arange(part_count, dtype=jnp.int32)[None, :]
    ).reshape(-1)
    source_slot = jnp.sum(
        jnp.where(wanted[:, None] == slot_iota[None, :], inverse[None, :], 0), axis=1
    ).reshape(ep_count, local_slots * part_count)
    partner = ep_index + 1 - 2 * (ep_index % 2)
    idx = jnp.concatenate(
        [
            lax.dynamic_index_in_dim(source_slot, ep_index, 0, keepdims=False),
            lax.dynamic_index_in_dim(source_slot, partner, 0, keepdims=False),
        ]
    ).astype(jnp.int32)
    model_rows = part_count * piece_rows
    raw_gate, raw_up, raw_down = (
        o.reshape(local_slots, model_rows, quarter_width)
        for o in relay(idx, (train_gate, train_up, train_down), ep_count, part_count)
    )

    step_count, tok_count, model_width = tokens.shape
    topk_count = route_ids.shape[2]
    capacity = (MOST + 1) // 2
    depth = capacity * step_count
    peer_rows = depth * local_slots
    all_tokens = step_count * tok_count
    same_slot = serve_place[:, None] == serve_place[None, :]
    replica_rank = jnp.sum(same_slot & (slot_iota[None, :] < slot_iota[:, None]), axis=1)
    pair_count = tok_count * topk_count
    pair_iota = jnp.arange(pair_count, dtype=jnp.int32)

    def rows(ids, decode_step):
        pair_experts = ids.reshape(pair_count)
        holders = serve_place[None, :] == pair_experts[:, None]
        replica_count = jnp.sum(holders, axis=1)
        earlier_pairs = (pair_experts[:, None] == pair_experts[None, :]) & (
            pair_iota[None, :] < pair_iota[:, None]
        )
        seen = jnp.sum(earlier_pairs, axis=1)
        target = (seen + ep_index) % replica_count
        position = seen // replica_count
        chosen = holders & (replica_rank[None, :] == target[:, None])
        dest_slot = jnp.sum(jnp.where(chosen, slot_iota[None, :], 0), axis=1)
        return (
            dest_slot // local_slots * peer_rows
            + (decode_step * capacity + position) * local_slots
            + dest_slot % local_slots
        )

    row_index = jax.vmap(rows)(route_ids, jnp.arange(step_count, dtype=jnp.int32))
    row_index = row_index.reshape(1, all_tokens, topk_count)
    buffer_iota = jnp.arange(ep_count * peer_rows, dtype=jnp.int32)
    placing = row_index == buffer_iota[:, None, None]
    mixing = jnp.sum(
        jnp.where(placing, route_weights.reshape(1, all_tokens, topk_count), 0.0), axis=2
    )
    send_rows = jnp.dot(
        jnp.any(placing, axis=2).astype(jnp.bfloat16),
        tokens.reshape(all_tokens, model_width),
        preferred_element_type=jnp.float32,
    ).astype(jnp.bfloat16)
    received = lax.all_to_all(
        send_rows.reshape(ep_count, depth, local_slots, model_width),
        "ep", split_axis=0, concat_axis=0, tiled=True,
    ).reshape(ep_count * depth, local_slots, model_width)
    mix = lax.all_to_all(
        mixing.reshape(ep_count, peer_rows, all_tokens),
        "ep", split_axis=0, concat_axis=0, tiled=True,
    )
    gate_act = jnp.einsum("mld,ldf->lmf", received, raw_gate, preferred_element_type=jnp.float32)
    up_act = jnp.einsum("mld,ldf->lmf", received, raw_up, preferred_element_type=jnp.float32)
    hidden = (jax.nn.silu(gate_act) * up_act).astype(jnp.bfloat16)
    partial_value = jnp.einsum(
        "lmf,ldf->lmd", hidden, raw_down, preferred_element_type=jnp.float32
    ).astype(jnp.bfloat16)
    mix = mix.reshape(ep_count, depth, local_slots, all_tokens)
    mix_high = mix.astype(jnp.bfloat16)
    mix_low = (mix - mix_high.astype(jnp.float32)).astype(jnp.bfloat16)
    rows_out = partial_value.reshape(local_slots, ep_count, depth, model_width)

    def combine(part):
        return jnp.einsum("pclt,lpcd->ptd", part, rows_out, preferred_element_type=jnp.float32)

    combined = (combine(mix_high) + combine(mix_low)).astype(jnp.bfloat16)
    combined = lax.optimization_barrier(combined)
    summed = lax.psum_scatter(combined, "tp", scatter_dimension=2, tiled=True)
    raw_gate, raw_up, raw_down, _ = lax.optimization_barrier(
        (raw_gate, raw_up, raw_down, combined)
    )
    serve_gate, serve_up, serve_down = (settle(o) for o in (raw_gate, raw_up, raw_down))
    summed, serve_gate, serve_up = lax.optimization_barrier((summed, serve_gate, serve_up))
    returned = lax.all_to_all(summed, "ep", split_axis=0, concat_axis=0, tiled=True)
    moe_out = jnp.sum(returned.astype(jnp.float32), axis=0).astype(jnp.bfloat16)
    moe_out = moe_out.reshape(step_count, tok_count, model_width // tp_count)
    return (serve_gate, serve_up, serve_down, moe_out)


def stream_kernel(
    levels, cap, cap_x, buffers, idx_ref, tok_ref, mix_ref, t0, t1, t2, o0, o1, o2, part_ref,
    firsts, lows, highs, crosses, ups, downs, across, stage, tokens, mix, acc, hid, flipped,
    load_sem, first_send, first_recv, up_send, up_recv, down_send, down_recv,
    across_send, cross_recv, cross_load, out_sem, tok_send, tok_recv, mix_send, mix_recv,
    here_sem, credit_first, credit_up, credit_down, credit_cross,
):
    trains, outs = (t0, t1, t2), (o0, o1, o2)
    me = lax.axis_index("ep")
    ep_count = 2 * levels
    z, x = lax.div(me, 2), lax.rem(me, 2)
    partner = me + 1 - 2 * x
    above, below = me + 2, me - 2
    local, _, half, width = t0.shape
    layer = 2 * local
    chunk = ups.shape[2]
    steps = half // chunk
    total = len(trains) * steps
    parts = stage.shape[1] // local
    depth = parts * 2 * chunk
    cross_slots = len(crosses)
    first_slots = firsts.shape[0]
    stages = stage.shape[0]
    group = depth // chunk
    tok_rows = tok_ref.shape[0]
    up_at, down_at = 0, UP_ROOM
    cross_at = 2 * UP_ROOM
    own_at = cross_at + parts * local
    other_at = own_at + parts * local
    high_at = 3 * parts * local
    has_up, has_down = z < levels - 1, z > 0

    def to(device):
        return {"device_id": {"ep": device}, "device_id_type": MESH}

    barrier = pltpu.get_barrier_semaphore()

    def greet(k, carry):
        pl.semaphore_signal(barrier, inc=1, **to(lax.rem(me + k, ep_count)))
        return carry

    lax.fori_loop(1, ep_count, greet, 0)
    pl.semaphore_wait(barrier, ep_count - 1)

    def rows_of(step):
        return pl.ds(pl.multiple_of(step * chunk, chunk), chunk)

    def tok_copy(k):
        return pltpu.make_async_remote_copy(
            src_ref=tok_ref,
            dst_ref=tokens.at[pl.ds(pl.multiple_of(me * tok_rows, 16), tok_rows)],
            send_sem=tok_send.at[k],
            recv_sem=tok_recv.at[k],
            **to(lax.rem(me + k, ep_count)),
        )

    def mix_copy(k):
        peer = lax.rem(me + k, ep_count)
        return pltpu.make_async_remote_copy(
            src_ref=mix_ref.at[peer],
            dst_ref=mix.at[pl.ds(pl.multiple_of(me * tok_rows, 16), tok_rows)],
            send_sem=mix_send.at[k],
            recv_sem=mix_recv.at[k],
            **to(peer),
        )

    def tok_here():
        return pltpu.make_async_copy(
            tok_ref, tokens.at[pl.ds(pl.multiple_of(me * tok_rows, 16), tok_rows)], here_sem.at[0]
        )

    def mix_here():
        return pltpu.make_async_copy(
            mix_ref.at[me], mix.at[pl.ds(pl.multiple_of(me * tok_rows, 16), tok_rows)],
            here_sem.at[1],
        )

    def load_copy(train, step, slot):
        return pltpu.make_async_copy(
            train.at[:, x, rows_of(step), :],
            firsts.at[slot, pl.ds(x * local, local)],
            load_sem.at[slot],
        )

    def first_copy(train, step, slot):
        return pltpu.make_async_remote_copy(
            src_ref=train.at[:, 1 - x, rows_of(step), :],
            dst_ref=firsts.at[slot, pl.ds(x * local, local)],
            send_sem=first_send.at[slot],
            recv_sem=first_recv.at[slot],
            **to(partner),
        )

    def own_cross_copy(train, step, slot):
        return pltpu.make_async_copy(
            train.at[:, 1 - x, rows_of(step), :], crosses[slot].at[pl.ds(0, local)],
            cross_load.at[slot],
        )

    def up_copy(side, slot):
        return pltpu.make_async_remote_copy(
            src_ref=ups.at[side],
            dst_ref=lows[slot].at[pl.ds(layer, cap)],
            send_sem=up_send.at[side],
            recv_sem=up_recv.at[slot],
            **to(above),
        )

    def down_copy(side, slot):
        return pltpu.make_async_remote_copy(
            src_ref=downs.at[side],
            dst_ref=highs[slot].at[pl.ds(layer, cap)],
            send_sem=down_send.at[side],
            recv_sem=down_recv.at[slot],
            **to(below),
        )

    def across_copy(side, slot):
        return pltpu.make_async_remote_copy(
            src_ref=across.at[side],
            dst_ref=crosses[slot].at[pl.ds(local, cap_x)],
            send_sem=across_send.at[side],
            recv_sem=cross_recv.at[slot],
            **to(partner),
        )

    def out_copy(out, step, place):
        return pltpu.make_async_copy(
            stage.at[place], out.at[:, :, rows_of(step), :], out_sem.at[place]
        )

    def each_array(n, action):
        for a in range(len(trains)):

            @pl.when((n >= a * steps) & (n < (a + 1) * steps))
            def _():
                action(a, n - a * steps)

    def each_slot(n, count, action):
        for b in range(count):

            @pl.when(lax.rem(n, count) == b)
            def _():
                action(b)

    def gather(count, put, take):
        wide = 4

        def several(g, carry):
            for k in range(wide):
                put(g * wide + k, take(g * wide + k))
            return carry

        lax.fori_loop(0, count // wide, several, 0)
        for j in range(count // wide * wide, count):
            put(j, take(j))

    def start(n):
        slot = lax.rem(n, first_slots)

        @pl.when(n >= first_slots)
        def _():
            pl.semaphore_wait(credit_first, 1)

        def go(a, step):
            first_copy(trains[a], step, slot).start()
            load_copy(trains[a], step, slot).start()

        each_array(n, go)

    def settle_first(n):
        place = lax.rem(n, first_slots)
        load_copy(t0, 0, place).wait()
        first_copy(t0, 0, place).wait()

        def go(slot):
            def both(j, value):
                lows[slot][j] = value
                highs[slot][j] = value

            gather(layer, both, lambda j: firsts[place, j])

        each_slot(n, buffers, go)

        @pl.when(n < total - first_slots)
        def _():
            pl.semaphore_signal(credit_first, inc=1, **to(partner))

    def send_up(n):
        side = lax.rem(n, 2)

        @pl.when(has_up & (n >= 2))
        def _():
            up_copy(side, 0).wait_send()

        def put(j, value):
            ups[side, j] = value

        def go(slot):
            @pl.when(has_down)
            def _():
                up_copy(side, slot).wait_recv()

            @pl.when(has_up)
            def _():
                gather(cap, put, lambda j: lows[slot][idx_ref[up_at + j]])

                @pl.when(n >= buffers)
                def _():
                    pl.semaphore_wait(credit_up, 1)

                up_copy(side, slot).start()

        each_slot(n, buffers, go)

    def send_down(n):
        side = lax.rem(n, 2)

        @pl.when(has_down & (n >= 2))
        def _():
            down_copy(side, 0).wait_send()

        def put(j, value):
            downs[side, j] = value

        def go(slot):
            @pl.when(has_up)
            def _():
                down_copy(side, slot).wait_recv()

            @pl.when(has_down)
            def _():
                gather(cap, put, lambda j: highs[slot][idx_ref[down_at + j]])

                @pl.when(n >= buffers)
                def _():
                    pl.semaphore_wait(credit_down, 1)

                down_copy(side, slot).start()

        each_slot(n, buffers, go)

    def send_across(n):
        side = lax.rem(n, 2)
        place = lax.rem(n, stages)

        @pl.when(n >= 2)
        def _():
            across_copy(side, 0).wait_send()

        def put(j, value):
            across[side, j] = value

        def either(slot, j):
            high = idx_ref[j + high_at]
            return jnp.where(high > 0, highs[slot][high], lows[slot][idx_ref[j]])

        def pack(slot):
            gather(cap_x, put, lambda j: either(slot, cross_at + j))

        each_slot(n, buffers, pack)

        @pl.when(n >= cross_slots)
        def _():
            pl.semaphore_wait(credit_cross, 1)

        each_slot(n, cross_slots, lambda b: across_copy(side, b).start())

        @pl.when(n >= stages)
        def _():
            out_copy(o0, 0, place).wait()

        def keep(j, value):
            stage[place, j, x] = value

        def own(slot):
            gather(parts * local, keep, lambda j: either(slot, own_at + j))

        each_slot(n, buffers, own)

        @pl.when(n < total - buffers)
        def _():
            @pl.when(has_up)
            def _():
                pl.semaphore_signal(credit_down, inc=1, **to(above))

            @pl.when(has_down)
            def _():
                pl.semaphore_signal(credit_up, inc=1, **to(below))

    def load_cross(n):
        def go(slot, a, step):
            own_cross_copy(trains[a], step, slot).start()

        each_slot(n, cross_slots, lambda b: each_array(n, functools.partial(go, b)))

    def slot_weights(place, s):
        rows = stage[place, pl.ds(s * parts, parts)]
        return rows.reshape(depth, width)

    def finish(n):
        place = lax.rem(n, stages)
        step = lax.rem(n, steps)

        def keep(j, value):
            stage[place, j, 1 - x] = value

        def other(slot):
            across_copy(0, slot).wait_recv()
            own_cross_copy(t0, 0, slot).wait()
            gather(parts * local, keep, lambda j: crosses[slot][idx_ref[other_at + j]])

        each_slot(n, cross_slots, other)
        each_array(n, lambda a, at: out_copy(outs[a], at, place).start())

        @pl.when(n < total - cross_slots)
        def _():
            pl.semaphore_signal(credit_cross, inc=1, **to(partner))

        @pl.when(n == 0)
        def _():
            tok_here().wait()
            mix_here().wait()

            def arrive(k, carry):
                tok_copy(k).wait()
                mix_copy(k).wait()
                return carry

            lax.fori_loop(1, ep_count, arrive, 0)

        @pl.when(n < 2 * steps)
        def _():
            which = lax.div(n, steps)
            lhs = tokens[:, pl.ds(pl.multiple_of(step * depth, depth), depth)]

            def add(s, carry):
                acc[which, s] += jnp.dot(
                    lhs, slot_weights(place, s), preferred_element_type=jnp.float32
                )
                return carry

            lax.fori_loop(0, local, add, 0)

        @pl.when(n == 2 * steps)
        def _():
            block = 128
            lane = lax.broadcasted_iota(jnp.int32, (block, mix.shape[1]), 1)

            def act(i, carry):
                s, b = lax.div(i, tokens.shape[0] // block), lax.rem(i, tokens.shape[0] // block)
                span = pl.ds(pl.multiple_of(b * block, block), block)
                scale = jnp.sum(jnp.where(lane == s, mix[span, :], 0.0), axis=1, keepdims=True)
                gate = acc[0, s, span, :]
                value = gate / (1.0 + jnp.exp(-gate)) * acc[1, s, span, :] * scale
                hid[s, :, span] = value.T.astype(jnp.bfloat16)
                return carry

            lax.fori_loop(0, local * (tokens.shape[0] // block), act, 0)

        @pl.when(n >= 2 * steps)
        def _():
            def add(s, carry):
                return carry + jnp.dot(
                    slot_weights(place, s), hid[s], preferred_element_type=jnp.float32
                )

            mixed = lax.fori_loop(
                0, local, add, jnp.zeros((depth, tokens.shape[0]), jnp.float32)
            )
            inner = lax.rem(step, group)
            for k in range(2 * parts):
                flipped[k, pl.ds(pl.multiple_of(inner * chunk, chunk), chunk), :] = mixed[
                    k * chunk : (k + 1) * chunk
                ]

            @pl.when(inner == group - 1)
            def _():
                for k in range(2 * parts):
                    at = pl.multiple_of(lax.div(step, group) * depth, depth)
                    part_ref[k, :, pl.ds(at, depth)] = flipped[k].T.astype(jnp.bfloat16)

    def spread(k, carry):
        tok_copy(k).start()
        mix_copy(k).start()
        return carry

    lax.fori_loop(1, ep_count, spread, 0)
    tok_here().start()
    mix_here().start()

    def clear(s, carry):
        for a in range(2):
            acc[a, s] = jnp.zeros(acc.shape[2:], jnp.float32)
        return carry

    def within(n):
        return (n >= 0) & (n < total)

    def iteration(i, carry):
        @pl.when(i < total)
        def _():
            start(i)

        @pl.when(within(i - 1))
        def _():
            settle_first(i - 1)

        n_up = i - 1 - z

        @pl.when(within(n_up))
        def _():
            send_up(n_up)

        n_down = i - levels + z

        @pl.when(within(n_down))
        def _():
            send_down(n_down)

        @pl.when(within(i - levels + 1))
        def _():
            load_cross(i - levels + 1)

        @pl.when(within(i - levels))
        def _():
            send_across(i - levels)

        @pl.when(i == 0)
        def _():
            lax.fori_loop(0, local, clear, 0)

        @pl.when(within(i - levels - 1))
        def _():
            finish(i - levels - 1)

        return carry

    lax.fori_loop(0, total + levels + 1, iteration, 0)
    for n in range(total - 2, total):

        @pl.when(has_up)
        def _():
            up_copy(n % 2, 0).wait_send()

        @pl.when(has_down)
        def _():
            down_copy(n % 2, 0).wait_send()

        across_copy(n % 2, 0).wait_send()
    for n in range(total - stages, total):
        out_copy(o0, 0, n % stages).wait()


def stream(idx, tok, mix, trains, ep_count, part_count, cap, collective):
    local, _, half, width = trains[0].shape
    levels = ep_count // 2
    chunk = 16
    buffers = levels + 3
    cross_slots = 4
    stages = 3
    picks = local * part_count
    cap_x = min(cap - local, picks)
    all_tokens = ep_count * tok.shape[0]
    depth = 2 * part_count * chunk
    dma = pltpu.SemaphoreType.DMA
    any_spec = pl.BlockSpec(memory_space=pl.ANY)
    bf16, f32 = jnp.bfloat16, jnp.float32
    return pl.pallas_call(
        functools.partial(stream_kernel, levels, cap, cap_x, buffers),
        out_shape=[jax.ShapeDtypeStruct((picks, 2, half, width), bf16)] * 3
        + [jax.ShapeDtypeStruct((2 * part_count, all_tokens, half), bf16)],
        in_specs=[pl.BlockSpec(memory_space=pltpu.SMEM)] + [any_spec] * 5,
        out_specs=[any_spec] * 3 + [pl.BlockSpec(memory_space=pltpu.VMEM)],
        scratch_shapes=[
            pltpu.VMEM((4, 2 * local, chunk, width), bf16),
            [pltpu.VMEM((2 * local + cap, chunk, width), bf16)] * buffers,
            [pltpu.VMEM((2 * local + cap, chunk, width), bf16)] * buffers,
            [pltpu.VMEM((local + cap_x, chunk, width), bf16)] * cross_slots,
            pltpu.VMEM((2, cap, chunk, width), bf16),
            pltpu.VMEM((2, cap, chunk, width), bf16),
            pltpu.VMEM((2, cap_x, chunk, width), bf16),
            pltpu.VMEM((stages, picks, 2, chunk, width), bf16),
            pltpu.VMEM((all_tokens, tok.shape[1]), bf16),
            pltpu.VMEM((all_tokens, mix.shape[2]), f32),
            pltpu.VMEM((2, local, all_tokens, width), f32),
            pltpu.VMEM((local, width, all_tokens), bf16),
            pltpu.VMEM((2 * part_count, depth, all_tokens), f32),
            dma((4,)),
            dma((4,)),
            dma((4,)),
            dma((2,)),
            dma((buffers,)),
            dma((2,)),
            dma((buffers,)),
            dma((2,)),
            dma((cross_slots,)),
            dma((cross_slots,)),
            dma((stages,)),
            dma((ep_count,)),
            dma((ep_count,)),
            dma((ep_count,)),
            dma((ep_count,)),
            dma((2,)),
            pltpu.SemaphoreType.REGULAR,
            pltpu.SemaphoreType.REGULAR,
            pltpu.SemaphoreType.REGULAR,
            pltpu.SemaphoreType.REGULAR,
        ],
        compiler_params=pltpu.CompilerParams(
            collective_id=collective, has_side_effects=True, vmem_limit_bytes=56 * 2**20
        ),
    )(idx, tok, mix, *trains)


def routing(train_map, serve_place, ep_index, ep_count, local, parts):
    slots = train_map.shape[0]
    levels = ep_count // 2
    layer = 2 * local
    held = jnp.arange(slots, dtype=jnp.int32)
    level, owner = held // layer, held // local
    devices = jnp.arange(ep_count, dtype=jnp.int32)
    floors = jnp.arange(levels, dtype=jnp.int32)
    wanted = serve_place.reshape(ep_count, local)
    need = jnp.any(wanted[:, :, None] == (train_map // parts)[None, None, :], axis=1)
    need_level = jnp.any(need.reshape(levels, 2, slots), axis=1)
    higher = floors[None, :, None] > floors[:, None, None]
    lower = floors[None, :, None] < floors[:, None, None]
    up = jnp.any(higher & need_level[None], axis=1) & (level[None, :] <= floors[:, None])
    down = jnp.any(lower & need_level[None], axis=1) & (level[None, :] >= floors[:, None])
    partner_need = need.reshape(levels, 2, slots)[:, ::-1].reshape(ep_count, slots)
    partners = devices + 1 - 2 * (devices % 2)
    cross = partner_need & (owner[None, :] != partners[:, None])
    flags = jnp.concatenate([up, down, cross], axis=0)
    before = (held[:, None] < held[None, :]).astype(jnp.bfloat16)
    place = jnp.dot(
        flags.astype(jnp.bfloat16), before, preferred_element_type=jnp.float32
    ).astype(jnp.int32)
    counts = jnp.sum(flags.astype(jnp.int32), axis=1)
    needed = jnp.maximum(
        jnp.max(counts[: 2 * levels]), jnp.max(counts[2 * levels :]) + local
    )

    def tables():
        z = ep_index // 2
        partner = ep_index + 1 - 2 * (ep_index % 2)

        def row(array, at):
            return lax.dynamic_index_in_dim(array, at, 0, keepdims=False)

        from_below = row(place, jnp.maximum(z - 1, 0))
        from_above = row(place, levels + jnp.minimum(z + 1, levels - 1))
        from_partner = row(place, 2 * levels + partner)
        here = held - layer * z
        where_low = jnp.where(level == z, here, jnp.where(level < z, layer + from_below, 0))
        where_high = jnp.where(level > z, layer + from_above, 0)
        where_cross = jnp.where(owner == ep_index, held - local * ep_index, local + from_partner)

        def listed(at, room, where):
            hit = row(flags, at)[None, :] & (
                row(place, at)[None, :] == jnp.arange(room, dtype=jnp.int32)[:, None]
            )
            return jnp.sum(jnp.where(hit, where[None, :], 0), axis=1)

        mine = (
            row(wanted, ep_index)[:, None] * parts + jnp.arange(parts, dtype=jnp.int32)[None, :]
        ).reshape(-1)
        same = mine[:, None] == train_map[None, :]
        def picked(where):
            return jnp.sum(jnp.where(same, where[None, :], 0), axis=1)

        room, at = parts * local, 2 * levels + ep_index
        return jnp.concatenate(
            [
                listed(z, UP_ROOM, where_low),
                listed(levels + z, UP_ROOM, where_high + jnp.where(level == z, here, 0)),
                listed(at, room, where_low),
                picked(where_low),
                picked(where_cross),
                listed(at, room, where_high),
                picked(where_high),
            ]
        ).astype(jnp.int32)

    return needed, tables


def stream_body(
    tokens, route_ids, route_weights, train_map, serve_place, train_gate, train_up, train_down
):
    ep_count = lax.axis_size("ep")
    tp_count = lax.axis_size("tp")
    ep_index = lax.axis_index("ep")
    slot_count = serve_place.shape[0]
    local, piece_rows, width = train_gate.shape
    parts = slot_count // EXPERTS
    step_count, tok_count, model_width = tokens.shape
    topk_count = route_ids.shape[2]
    rows = step_count * tok_count
    half, chunk = piece_rows // 2, 16
    full = slot_count - 2 * local
    caps = [c for c in CAPS if c < full] + [full]

    slot_iota = jnp.arange(slot_count, dtype=jnp.int32)
    first = ~jnp.any(
        (serve_place[:, None] == serve_place[None, :]) & (slot_iota[None, :] < slot_iota[:, None]),
        axis=1,
    )
    holder = jnp.where(first, serve_place, -1)
    ids = route_ids.reshape(rows, topk_count)
    weights = route_weights.reshape(rows, topk_count)
    mix = jnp.sum(
        jnp.where(ids[:, :, None] == holder[None, None, :], weights[:, :, None], 0.0), axis=1
    )
    mix = mix.reshape(rows, ep_count, local).transpose(1, 0, 2)
    mix = jnp.pad(mix, ((0, 0), (0, 0), (0, 128 - local)))
    ordered = (
        tokens.reshape(rows, 2 * parts, half // chunk, chunk)
        .transpose(0, 2, 1, 3)
        .reshape(rows, model_width)
    )
    needed, tables = routing(train_map, serve_place, ep_index, ep_count, local, parts)
    choice = sum((needed > c).astype(jnp.int32) for c in caps[:-1])
    idx = tables()
    trains = [t.reshape(local, 2, half, width) for t in (train_gate, train_up, train_down)]

    def run(collective, cap_static):
        def branch(idx, ordered, mix, *trains):
            return tuple(
                stream(idx, ordered, mix, trains, ep_count, parts, cap_static, collective)
            )

        return branch

    raw_gate, raw_up, raw_down, combined = lax.switch(
        choice, [run(k, c) for k, c in enumerate(caps)], idx, ordered, mix, *trains
    )
    raw_gate, raw_up, raw_down = (
        o.reshape(local, model_width, width) for o in (raw_gate, raw_up, raw_down)
    )
    blocks = 2 * parts // tp_count
    spread = lax.all_to_all(combined, "tp", split_axis=0, concat_axis=0, tiled=True)
    serve_gate, serve_up = settle(raw_gate), settle(raw_up)
    spread, serve_gate, serve_up = lax.optimization_barrier((spread, serve_gate, serve_up))
    spread = spread.reshape(tp_count, blocks, ep_count, rows, half).astype(jnp.float32)
    summed = jnp.sum(spread, axis=0).astype(jnp.bfloat16).transpose(1, 0, 2, 3)
    returned = lax.all_to_all(summed, "ep", split_axis=0, concat_axis=0, tiled=True)
    serve_down = settle(raw_down)
    returned, serve_down = lax.optimization_barrier((returned, serve_down))
    moe_out = jnp.sum(returned.astype(jnp.float32), axis=0).astype(jnp.bfloat16)
    moe_out = moe_out.transpose(1, 0, 2).reshape(
        step_count, tok_count, model_width // tp_count
    )
    return (serve_gate, serve_up, serve_down, moe_out)


def settle_kernel(source, target):
    target[...] = source[...]


def settle(source):
    slots, rows, width = source.shape
    spec = pl.BlockSpec((1, rows, width), lambda i: (i, 0, 0))
    return pl.pallas_call(
        settle_kernel,
        grid=(slots,),
        out_shape=jax.ShapeDtypeStruct(source.shape, source.dtype),
        in_specs=[spec],
        out_specs=spec,
        cost_estimate=pl.CostEstimate(
            flops=0, bytes_accessed=4 * slots * rows * width, transcendentals=0
        ),
    )(source)


def solution(mesh):
    in_specs = (
        P(None, "ep", None),
        P(None, "ep", None),
        P(None, "ep", None),
        P(),
        P(),
        P("ep", None, "tp"),
        P("ep", None, "tp"),
        P("ep", None, "tp"),
    )
    out_specs = (P("ep", None, "tp"), P("ep", None, "tp"), P("ep", None, "tp"), P(None, "ep", "tp"))
    chosen = stream_body if mesh.shape["ep"] <= 8 else body
    return jax.shard_map(chosen, mesh=mesh, in_specs=in_specs, out_specs=out_specs, check_vma=False)
```

```python
import functools

import jax
import jax.numpy as jnp
from jax import lax
from jax.experimental import pallas as pl
from jax.experimental.pallas import tpu as pltpu
from jax.sharding import PartitionSpec as P

EXPERTS = 16
MOST = 10
MESH = pl.DeviceIdType.MESH
CAPS = (32, 33, 34, 35, 37)
ROOM = 48
CHOICES = 2048
SPAN = 128
HOP = 2
AHEAD = 2


def relay_kernel(
    pairs, chunk_rows, buffers, idx_ref, t0, t1, t2, o0, o1, o2, held, whole, own, other,
    local_sem, first_send, first_recv, line_send, line_recv,
    own_sem, other_send, other_recv, stage_sem, credit_x, credit_up, credit_down,
):
    trains, outs = (t0, t1, t2), (o0, o1, o2)
    me = lax.axis_index("ep")
    z, x = lax.div(me, 2), lax.rem(me, 2)
    partner = me + 1 - 2 * x
    above, below = me + 2, me - 2
    local = t0.shape[0]
    half = t0.shape[1] // 2
    steps = half // chunk_rows
    total = len(trains) * steps
    layer = 2 * local
    picks = own.shape[1]
    recv_slots = other_recv.shape[0]
    has_up, has_down = z < pairs - 1, z > 0

    barrier = pltpu.get_barrier_semaphore()
    pl.semaphore_signal(barrier, inc=1, device_id={"ep": partner}, device_id_type=MESH)

    @pl.when(has_up)
    def _():
        pl.semaphore_signal(barrier, inc=1, device_id={"ep": above}, device_id_type=MESH)

    @pl.when(has_down)
    def _():
        pl.semaphore_signal(barrier, inc=1, device_id={"ep": below}, device_id_type=MESH)

    pl.semaphore_wait(barrier, 1 + jnp.where(has_up, 1, 0) + jnp.where(has_down, 1, 0))

    def rows_of(side, step):
        return pl.ds(pl.multiple_of(side * half + step * chunk_rows, chunk_rows), chunk_rows)

    def mine(slot):
        return held.at[slot, pl.ds(me * local, local)]

    def region(slot, level):
        return held.at[slot, pl.ds(level * layer, layer)]

    def load_copy(train, step, slot):
        return pltpu.make_async_copy(
            train.at[:, rows_of(x, step), :], mine(slot), local_sem.at[slot]
        )

    def first_copy(train, step, slot):
        return pltpu.make_async_remote_copy(
            src_ref=train.at[:, rows_of(1 - x, step), :],
            dst_ref=mine(slot),
            send_sem=first_send.at[slot],
            recv_sem=first_recv.at[slot],
            device_id={"ep": partner},
            device_id_type=MESH,
        )

    def up_copy(slot, level):
        return pltpu.make_async_remote_copy(
            src_ref=region(slot, level),
            dst_ref=region(slot, level),
            send_sem=line_send.at[slot, level],
            recv_sem=line_recv.at[slot, level],
            device_id={"ep": above},
            device_id_type=MESH,
        )

    def down_copy(slot, level):
        return pltpu.make_async_remote_copy(
            src_ref=region(slot, level),
            dst_ref=region(slot, level),
            send_sem=line_send.at[slot, level + 1],
            recv_sem=line_recv.at[slot, level],
            device_id={"ep": below},
            device_id_type=MESH,
        )

    def own_copy(out, step, stage):
        return pltpu.make_async_copy(
            own.at[stage], out.at[:, rows_of(x, step), :], own_sem.at[stage]
        )

    def other_copy(out, step, stage, recv_slot):
        return pltpu.make_async_remote_copy(
            src_ref=other.at[stage],
            dst_ref=out.at[:, rows_of(x, step), :],
            send_sem=other_send.at[stage],
            recv_sem=other_recv.at[recv_slot],
            device_id={"ep": partner},
            device_id_type=MESH,
        )

    def stage_start(n):
        slot = lax.rem(n, buffers)

        @pl.when(n >= buffers)
        def _():
            pl.semaphore_wait(credit_x, 1)

        for a in range(len(trains)):

            @pl.when((n >= a * steps) & (n < (a + 1) * steps))
            def _():
                first_copy(trains[a], n - a * steps, slot).start()
                load_copy(trains[a], n - a * steps, slot).start()

    def stage_send(n):
        slot = lax.rem(n, buffers)
        load_copy(t0, 0, slot).wait()
        first_copy(t0, 0, slot).wait()

        @pl.when(has_up)
        def _():
            @pl.when(n >= buffers)
            def _():
                pl.semaphore_wait(credit_up, 1)

            up_copy(slot, z).start()

        @pl.when(has_down)
        def _():
            @pl.when(n >= buffers)
            def _():
                pl.semaphore_wait(credit_down, 1)

            down_copy(slot, z).start()

    def stage_forward(n, distance):
        slot = lax.rem(n, buffers)

        @pl.when(z - distance >= 0)
        def _():
            up_copy(slot, z - distance).wait_recv()

            @pl.when(has_up)
            def _():
                up_copy(slot, z - distance).start()

        @pl.when(z + distance < pairs)
        def _():
            down_copy(slot, z + distance).wait_recv()

            @pl.when(has_down)
            def _():
                down_copy(slot, z + distance).start()

    def stage_finish(n):
        slot = lax.rem(n, buffers)
        stage = lax.rem(n, 2)
        taken = pltpu.make_async_copy(held.at[slot], whole, stage_sem)
        taken.start()

        def drain_up(level, carry):
            up_copy(slot, level).wait_send()
            return carry

        def drain_down(level, carry):
            down_copy(slot, level).wait_send()
            return carry

        @pl.when(has_up)
        def _():
            lax.fori_loop(0, z + 1, drain_up, 0)

        @pl.when(has_down)
        def _():
            lax.fori_loop(z, pairs, drain_down, 0)

        taken.wait()

        @pl.when(n < total - buffers)
        def _():
            pl.semaphore_signal(credit_x, inc=1, device_id={"ep": partner}, device_id_type=MESH)

            @pl.when(has_up)
            def _():
                pl.semaphore_signal(
                    credit_down, inc=1, device_id={"ep": above}, device_id_type=MESH
                )

            @pl.when(has_down)
            def _():
                pl.semaphore_signal(
                    credit_up, inc=1, device_id={"ep": below}, device_id_type=MESH
                )

        @pl.when(n >= 2)
        def _():
            own_copy(o0, 0, stage).wait()
            other_copy(o0, 0, stage, 0).wait_send()

        @pl.when(n >= 1)
        def _():
            other_copy(o0, 0, stage, lax.rem(n - 1, recv_slots)).wait_recv()

        def pick(s, carry):
            other[stage, s] = whole[idx_ref[picks + s]]
            own[stage, s] = whole[idx_ref[s]]
            return carry

        lax.fori_loop(0, picks, pick, 0)
        for a in range(len(trains)):

            @pl.when((n >= a * steps) & (n < (a + 1) * steps))
            def _():
                other_copy(outs[a], n - a * steps, stage, lax.rem(n, recv_slots)).start()
                own_copy(outs[a], n - a * steps, stage).start()

    def iteration(i, carry):
        @pl.when(i < total)
        def _():
            stage_start(i)

        @pl.when((i >= 1) & (i - 1 < total))
        def _():
            stage_send(i - 1)

        def hop(distance, inner):
            n = i - 1 - distance

            @pl.when((n >= 0) & (n < total))
            def _():
                stage_forward(n, distance)

            return inner

        lax.fori_loop(1, pairs, hop, 0)

        @pl.when(i >= pairs)
        def _():
            stage_finish(i - pairs)

        return carry

    lax.fori_loop(0, total + pairs, iteration, 0)
    for n in range(max(total - 2, 0), total):
        own_copy(o0, 0, n % 2).wait()
        other_copy(o0, 0, n % 2, 0).wait_send()
    other_copy(o0, 0, 0, (total - 1) % recv_slots).wait_recv()


def relay(idx, trains, ep_count, part_count):
    local, piece_rows, width = trains[0].shape
    pairs = ep_count // 2
    slots = ep_count * local
    buffers = pairs + 3
    chunk_rows = 32
    while chunk_rows > 16 and buffers * slots * chunk_rows * width * 2 > 24 * 2**20:
        chunk_rows //= 2
    picks = local * part_count
    dma = pltpu.SemaphoreType.DMA
    any_spec = pl.BlockSpec(memory_space=pl.ANY)
    return pl.pallas_call(
        functools.partial(relay_kernel, pairs, chunk_rows, buffers),
        out_shape=[jax.ShapeDtypeStruct((picks, piece_rows, width), jnp.bfloat16)] * 3,
        in_specs=[pl.BlockSpec(memory_space=pltpu.SMEM)] + [any_spec] * 3,
        out_specs=[any_spec] * 3,
        scratch_shapes=[
            pltpu.VMEM((buffers, slots, chunk_rows, width), jnp.bfloat16),
            pltpu.VMEM((slots, chunk_rows, width), jnp.bfloat16),
            pltpu.VMEM((2, picks, chunk_rows, width), jnp.bfloat16),
            pltpu.VMEM((2, picks, chunk_rows, width), jnp.bfloat16),
            dma((buffers,)),
            dma((buffers,)),
            dma((buffers,)),
            dma((buffers, pairs + 1)),
            dma((buffers, pairs)),
            dma((2,)),
            dma((2,)),
            dma((buffers + 2,)),
            dma,
            pltpu.SemaphoreType.REGULAR,
            pltpu.SemaphoreType.REGULAR,
            pltpu.SemaphoreType.REGULAR,
        ],
        compiler_params=pltpu.CompilerParams(
            collective_id=0, has_side_effects=True, vmem_limit_bytes=56 * 2**20
        ),
    )(idx, *trains)


def body(
    tokens, route_ids, route_weights, train_map, serve_place, train_gate, train_up, train_down
):
    ep_count = lax.axis_size("ep")
    tp_count = lax.axis_size("tp")
    ep_index = lax.axis_index("ep")
    slot_count = serve_place.shape[0]
    local_slots, piece_rows, quarter_width = train_gate.shape
    part_count = slot_count // EXPERTS
    slot_iota = jnp.arange(slot_count, dtype=jnp.int32)
    inverse = jnp.sum(
        jnp.where(train_map[:, None] == slot_iota[None, :], slot_iota[:, None], 0), axis=0
    )
    wanted = (
        serve_place[:, None] * part_count + jnp.arange(part_count, dtype=jnp.int32)[None, :]
    ).reshape(-1)
    source_slot = jnp.sum(
        jnp.where(wanted[:, None] == slot_iota[None, :], inverse[None, :], 0), axis=1
    ).reshape(ep_count, local_slots * part_count)
    partner = ep_index + 1 - 2 * (ep_index % 2)
    idx = jnp.concatenate(
        [
            lax.dynamic_index_in_dim(source_slot, ep_index, 0, keepdims=False),
            lax.dynamic_index_in_dim(source_slot, partner, 0, keepdims=False),
        ]
    ).astype(jnp.int32)
    model_rows = part_count * piece_rows
    raw_gate, raw_up, raw_down = (
        o.reshape(local_slots, model_rows, quarter_width)
        for o in relay(idx, (train_gate, train_up, train_down), ep_count, part_count)
    )

    step_count, tok_count, model_width = tokens.shape
    topk_count = route_ids.shape[2]
    capacity = (MOST + 1) // 2
    depth = capacity * step_count
    peer_rows = depth * local_slots
    all_tokens = step_count * tok_count
    same_slot = serve_place[:, None] == serve_place[None, :]
    replica_rank = jnp.sum(same_slot & (slot_iota[None, :] < slot_iota[:, None]), axis=1)
    pair_count = tok_count * topk_count
    pair_iota = jnp.arange(pair_count, dtype=jnp.int32)

    def rows(ids, decode_step):
        pair_experts = ids.reshape(pair_count)
        holders = serve_place[None, :] == pair_experts[:, None]
        replica_count = jnp.sum(holders, axis=1)
        earlier_pairs = (pair_experts[:, None] == pair_experts[None, :]) & (
            pair_iota[None, :] < pair_iota[:, None]
        )
        seen = jnp.sum(earlier_pairs, axis=1)
        target = (seen + ep_index) % replica_count
        position = seen // replica_count
        chosen = holders & (replica_rank[None, :] == target[:, None])
        dest_slot = jnp.sum(jnp.where(chosen, slot_iota[None, :], 0), axis=1)
        return (
            dest_slot // local_slots * peer_rows
            + (decode_step * capacity + position) * local_slots
            + dest_slot % local_slots
        )

    row_index = jax.vmap(rows)(route_ids, jnp.arange(step_count, dtype=jnp.int32))
    row_index = row_index.reshape(1, all_tokens, topk_count)
    buffer_iota = jnp.arange(ep_count * peer_rows, dtype=jnp.int32)
    placing = row_index == buffer_iota[:, None, None]
    mixing = jnp.sum(
        jnp.where(placing, route_weights.reshape(1, all_tokens, topk_count), 0.0), axis=2
    )
    send_rows = jnp.dot(
        jnp.any(placing, axis=2).astype(jnp.bfloat16),
        tokens.reshape(all_tokens, model_width),
        preferred_element_type=jnp.float32,
    ).astype(jnp.bfloat16)
    received = lax.all_to_all(
        send_rows.reshape(ep_count, depth, local_slots, model_width),
        "ep", split_axis=0, concat_axis=0, tiled=True,
    ).reshape(ep_count * depth, local_slots, model_width)
    mix = lax.all_to_all(
        mixing.reshape(ep_count, peer_rows, all_tokens),
        "ep", split_axis=0, concat_axis=0, tiled=True,
    )
    gate_act = jnp.einsum("mld,ldf->lmf", received, raw_gate, preferred_element_type=jnp.float32)
    up_act = jnp.einsum("mld,ldf->lmf", received, raw_up, preferred_element_type=jnp.float32)
    hidden = (jax.nn.silu(gate_act) * up_act).astype(jnp.bfloat16)
    partial_value = jnp.einsum(
        "lmf,ldf->lmd", hidden, raw_down, preferred_element_type=jnp.float32
    ).astype(jnp.bfloat16)
    mix = mix.reshape(ep_count, depth, local_slots, all_tokens)
    mix_high = mix.astype(jnp.bfloat16)
    mix_low = (mix - mix_high.astype(jnp.float32)).astype(jnp.bfloat16)
    rows_out = partial_value.reshape(local_slots, ep_count, depth, model_width)

    def combine(part):
        return jnp.einsum("pclt,lpcd->ptd", part, rows_out, preferred_element_type=jnp.float32)

    combined = (combine(mix_high) + combine(mix_low)).astype(jnp.bfloat16)
    combined = lax.optimization_barrier(combined)
    summed = lax.psum_scatter(combined, "tp", scatter_dimension=2, tiled=True)
    raw_gate, raw_up, raw_down, _ = lax.optimization_barrier(
        (raw_gate, raw_up, raw_down, combined)
    )
    serve_gate, serve_up, serve_down = (settle(o) for o in (raw_gate, raw_up, raw_down))
    summed, serve_gate, serve_up = lax.optimization_barrier((summed, serve_gate, serve_up))
    returned = lax.all_to_all(summed, "ep", split_axis=0, concat_axis=0, tiled=True)
    moe_out = jnp.sum(returned.astype(jnp.float32), axis=0).astype(jnp.bfloat16)
    moe_out = moe_out.reshape(step_count, tok_count, model_width // tp_count)
    return (serve_gate, serve_up, serve_down, moe_out)


def stream_kernel(
    levels, cap, hop, ahead, idx_ref, tok_ref, mix_ref, t0, t1, t2, o0, o1, o2, part_ref,
    mines, lows, highs, crosses, ups, downs, across, stage, tokens, mix, acc, hid, flipped,
    mine_sem, up_send, up_recv, down_send, down_recv, across_send, cross_recv, out_sem,
    tok_send, tok_recv, mix_send, mix_recv, here_sem, credit_up, credit_down, credit_cross,
):
    trains, outs = (t0, t1, t2), (o0, o1, o2)
    me = lax.axis_index("ep")
    ep_count = 2 * levels
    z, x = lax.div(me, 2), lax.rem(me, 2)
    partner = me + 1 - 2 * x
    above, below = me + 2, me - 2
    own, half, width = t0.shape
    chunk, span = ups.shape[2], ups.shape[3]
    splits = width // span
    steps = half // chunk
    per_array = steps * splits
    total = len(trains) * per_array
    picks = stage.shape[1]
    slots = hid.shape[0]
    depth = picks // slots * chunk
    layer = 2 * own
    buffers, mine_slots = len(lows), len(mines)
    cross_slots, stages = len(crosses), stage.shape[0]
    group = depth // chunk
    tok_rows = tok_ref.shape[0]
    up_at, down_at, first_at = 0, ROOM, 2 * ROOM
    cross_at = first_at + own
    pick_at = cross_at + 2 * ROOM
    has_up, has_down = z < levels - 1, z > 0
    travel = levels * hop

    def to(device):
        return {"device_id": {"ep": device}, "device_id_type": MESH}

    barrier = pltpu.get_barrier_semaphore()

    def greet(k, carry):
        pl.semaphore_signal(barrier, inc=1, **to(lax.rem(me + k, ep_count)))
        return carry

    lax.fori_loop(1, ep_count, greet, 0)
    pl.semaphore_wait(barrier, ep_count - 1)

    def my_rows(ref):
        return ref.at[pl.ds(pl.multiple_of(me * tok_rows, 16), tok_rows)]

    def tok_copy(k):
        return pltpu.make_async_remote_copy(
            src_ref=tok_ref,
            dst_ref=my_rows(tokens),
            send_sem=tok_send.at[k],
            recv_sem=tok_recv.at[k],
            **to(lax.rem(me + k, ep_count)),
        )

    def mix_copy(k):
        peer = lax.rem(me + k, ep_count)
        return pltpu.make_async_remote_copy(
            src_ref=mix_ref.at[peer],
            dst_ref=my_rows(mix),
            send_sem=mix_send.at[k],
            recv_sem=mix_recv.at[k],
            **to(peer),
        )

    def tok_here():
        return pltpu.make_async_copy(tok_ref, my_rows(tokens), here_sem.at[0])

    def mix_here():
        return pltpu.make_async_copy(mix_ref.at[me], my_rows(mix), here_sem.at[1])

    def part_of(array, at):
        step, column = lax.div(at, splits), lax.rem(at, splits)
        rows = pl.ds(pl.multiple_of(step * chunk, chunk), chunk)
        return array.at[:, rows, pl.ds(pl.multiple_of(column * span, span), span)]

    def mine_copy(train, at, slot):
        return pltpu.make_async_copy(part_of(train, at), mines[slot], mine_sem.at[slot])

    def up_copy(side, slot):
        return pltpu.make_async_remote_copy(
            src_ref=ups.at[side],
            dst_ref=lows[slot].at[pl.ds(layer, cap)],
            send_sem=up_send.at[side],
            recv_sem=up_recv.at[slot],
            **to(above),
        )

    def down_copy(side, slot):
        return pltpu.make_async_remote_copy(
            src_ref=downs.at[side],
            dst_ref=highs[slot].at[pl.ds(layer, cap)],
            send_sem=down_send.at[side],
            recv_sem=down_recv.at[slot],
            **to(below),
        )

    def across_copy(side, slot):
        return pltpu.make_async_remote_copy(
            src_ref=across.at[side],
            dst_ref=crosses[slot],
            send_sem=across_send.at[side],
            recv_sem=cross_recv.at[slot],
            **to(partner),
        )

    def out_copy(out, at, place):
        return pltpu.make_async_copy(stage.at[place], part_of(out, at), out_sem.at[place])

    def each_array(n, action):
        for a in range(len(trains)):

            @pl.when((n >= a * per_array) & (n < (a + 1) * per_array))
            def _():
                action(a, n - a * per_array)

    def each_slot(n, count, action):
        for b in range(count):

            @pl.when(lax.rem(n, count) == b)
            def _():
                action(b)

    def gather(start, stop, put, take):
        wide = 4

        def several(g, carry):
            for k in range(wide):
                put(start + g * wide + k, take(start + g * wide + k))
            return carry

        full = (stop - start) // wide
        lax.fori_loop(0, full, several, 0)
        for j in range(start + full * wide, stop):
            put(j, take(j))

    def load(n):
        def go(slot, a, at):
            mine_copy(trains[a], at, slot).start()

        each_slot(n, mine_slots, lambda b: each_array(n, functools.partial(go, b)))

    def either(slot, j, far):
        high = idx_ref[j + far]
        return jnp.where(high > 0, highs[slot][high], lows[slot][idx_ref[j]])

    def send_across(m):
        side = lax.rem(m, 2)
        n = m - travel

        @pl.when(m >= 2)
        def _():
            across_copy(side, 0).wait_send()

        def put(j, value):
            across[side, j] = value

        @pl.when(m < total)
        def _():
            def go(slot):
                mine_copy(t0, 0, slot).wait()
                gather(0, own, put, lambda j: mines[slot][jnp.maximum(idx_ref[first_at + j] - 1, 0)])

            each_slot(m, mine_slots, go)

        @pl.when(n >= 0)
        def _():
            def mixed(slot, j):
                is_first = idx_ref[first_at + j] > 0
                return jnp.where(is_first, across[side, j], either(slot, cross_at + j, ROOM))

            def go(slot):
                gather(0, own, put, functools.partial(mixed, slot))
                gather(own, cap, put, lambda j: either(slot, cross_at + j, ROOM))

            each_slot(n, buffers, go)

        @pl.when(m >= cross_slots)
        def _():
            pl.semaphore_wait(credit_cross, 1)

        each_slot(m, cross_slots, lambda b: across_copy(side, b).start())

    def take_first(n):
        def from_mine(slot, source):
            def both(j, value):
                lows[slot][j] = value
                highs[slot][j] = value

            gather(0, own, both, lambda j: mines[source][j])

        def from_partner(slot, source):
            def both(j, value):
                lows[slot][own + j] = value
                highs[slot][own + j] = value

            gather(0, own, both, lambda j: crosses[source][j])

        def go(slot):
            each_slot(n, mine_slots, functools.partial(from_mine, slot))
            each_slot(n, cross_slots, functools.partial(from_partner, slot))

        each_slot(n, buffers, go)

    def send_up(n):
        side = lax.rem(n, 2)

        @pl.when(has_up & (n >= 2))
        def _():
            up_copy(side, 0).wait_send()

        def put(j, value):
            ups[side, j] = value

        def go(slot):
            @pl.when(has_down)
            def _():
                up_copy(side, slot).wait_recv()

            @pl.when(has_up)
            def _():
                gather(0, cap, put, lambda j: lows[slot][idx_ref[up_at + j]])

                @pl.when(n >= buffers)
                def _():
                    pl.semaphore_wait(credit_up, 1)

                up_copy(side, slot).start()

        each_slot(n, buffers, go)

    def send_down(n):
        side = lax.rem(n, 2)

        @pl.when(has_down & (n >= 2))
        def _():
            down_copy(side, 0).wait_send()

        def put(j, value):
            downs[side, j] = value

        def go(slot):
            @pl.when(has_up)
            def _():
                down_copy(side, slot).wait_recv()

            @pl.when(has_down)
            def _():
                gather(0, cap, put, lambda j: highs[slot][idx_ref[down_at + j]])

                @pl.when(n >= buffers)
                def _():
                    pl.semaphore_wait(credit_down, 1)

                down_copy(side, slot).start()

        each_slot(n, buffers, go)

    def collect(n):
        place = lax.rem(n, stages)

        @pl.when(n >= stages)
        def _():
            out_copy(o0, 0, place).wait()

        def keep(j, value):
            stage[place, j] = value

        def go(slot):
            gather(0, picks, keep, lambda j: either(slot, pick_at + j, picks))

        each_slot(n, buffers, go)

        @pl.when(n < total - buffers)
        def _():
            @pl.when(has_up)
            def _():
                pl.semaphore_signal(credit_down, inc=1, **to(above))

            @pl.when(has_down)
            def _():
                pl.semaphore_signal(credit_up, inc=1, **to(below))

    def slot_weights(place, s):
        return stage[place, pl.ds(s * (picks // slots), picks // slots)].reshape(depth, span)

    def finish(n):
        place = lax.rem(n, stages)
        at = lax.rem(n, per_array)
        step, column = lax.div(at, splits), lax.rem(at, splits)
        columns = pl.ds(pl.multiple_of(column * span, span), span)

        def keep(j, value):
            stage[place, j] = value

        def other(slot):
            def take(j):
                there = idx_ref[pick_at + 2 * picks + j]
                return jnp.where(
                    there > 0, crosses[slot][jnp.maximum(there - 1, 0)], stage[place, j]
                )

            gather(0, picks, keep, take)

        each_slot(n + travel, cross_slots, other)
        each_array(n, lambda a, where: out_copy(outs[a], where, place).start())

        @pl.when(n == 0)
        def _():
            tok_here().wait()
            mix_here().wait()

            def arrive(k, carry):
                tok_copy(k).wait()
                mix_copy(k).wait()
                return carry

            lax.fori_loop(1, ep_count, arrive, 0)

        @pl.when(n < 2 * per_array)
        def _():
            which = lax.div(n, per_array)
            lhs = tokens[:, pl.ds(pl.multiple_of(step * depth, depth), depth)]

            def add(s, carry):
                acc[which, s, :, columns] += jnp.dot(
                    lhs, slot_weights(place, s), preferred_element_type=jnp.float32
                )
                return carry

            lax.fori_loop(0, slots, add, 0)

        @pl.when(n == 2 * per_array)
        def _():
            block = 128
            blocks = tokens.shape[0] // block
            lane = lax.broadcasted_iota(jnp.int32, (block, mix.shape[1]), 1)

            def act(i, carry):
                s, b = lax.div(i, blocks), lax.rem(i, blocks)
                rows = pl.ds(pl.multiple_of(b * block, block), block)
                scale = jnp.sum(jnp.where(lane == s, mix[rows, :], 0.0), axis=1, keepdims=True)
                gate = acc[0, s, rows, :]
                value = gate / (1.0 + jnp.exp(-gate)) * acc[1, s, rows, :] * scale
                hid[s, :, rows] = value.T.astype(jnp.bfloat16)
                return carry

            lax.fori_loop(0, slots * blocks, act, 0)

        @pl.when(n >= 2 * per_array)
        def _():
            def add(s, carry):
                return carry + jnp.dot(
                    slot_weights(place, s), hid[s, columns, :],
                    preferred_element_type=jnp.float32,
                )

            mixed = lax.fori_loop(0, slots, add, jnp.zeros((depth, tokens.shape[0]), jnp.float32))
            inner = lax.rem(step, group)
            rows = pl.ds(pl.multiple_of(inner * chunk, chunk), chunk)
            for k in range(group):
                piece = mixed[k * chunk : (k + 1) * chunk]
                before = jnp.where(column == 0, jnp.zeros_like(piece), flipped[k, rows, :])
                flipped[k, rows, :] = before + piece

            @pl.when((inner == group - 1) & (column == splits - 1))
            def _():
                for k in range(group):
                    place_at = pl.multiple_of(lax.div(step, group) * depth, depth)
                    part_ref[k, :, pl.ds(place_at, depth)] = flipped[k].T.astype(jnp.bfloat16)

    def spread(k, carry):
        tok_copy(k).start()
        mix_copy(k).start()
        return carry

    def clear(s, carry):
        for a in range(2):
            acc[a, s] = jnp.zeros(acc.shape[2:], jnp.float32)
        return carry

    def within(n):
        return (n >= 0) & (n < total)

    def iteration(i, carry):
        @pl.when(i < total)
        def _():
            load(i)

        @pl.when(i == 0)
        def _():
            lax.fori_loop(1, ep_count, spread, 0)
            tok_here().start()
            mix_here().start()
            lax.fori_loop(0, slots, clear, 0)

        m = i - ahead - hop
        arrived = (m >= 0) & (m < total + travel)

        @pl.when(arrived)
        def _():
            each_slot(m, cross_slots, lambda b: across_copy(0, b).wait_recv())

        @pl.when(within(m))
        def _():
            take_first(m)

        n_up = m - z * hop

        @pl.when(within(n_up))
        def _():
            send_up(n_up)

        n_down = m - (levels - 1 - z) * hop

        @pl.when(within(n_down))
        def _():
            send_down(n_down)

        @pl.when((i >= ahead) & (i - ahead < total + travel))
        def _():
            send_across(i - ahead)

        @pl.when(within(i - ahead - travel))
        def _():
            collect(i - ahead - travel)

        @pl.when(within(m - travel))
        def _():
            finish(m - travel)

        @pl.when(arrived & (m < total + travel - cross_slots))
        def _():
            pl.semaphore_signal(credit_cross, inc=1, **to(partner))

        return carry

    lax.fori_loop(0, total + travel + ahead + hop, iteration, 0)
    for n in range(2):

        @pl.when(has_up)
        def _():
            up_copy(n, 0).wait_send()

        @pl.when(has_down)
        def _():
            down_copy(n, 0).wait_send()

        across_copy(n, 0).wait_send()
    for n in range(stages):
        out_copy(o0, 0, n).wait()


def stream(idx, tok, mix, trains, ep_count, slots, cap, collective):
    own, half, width = trains[0].shape
    levels = ep_count // 2
    chunk, span = 16, SPAN
    hop, ahead = HOP, AHEAD
    buffers = (levels - 1) * hop + 4
    mine_slots = ahead + hop + 1
    cross_slots = hop + 3
    stages = hop + 3
    picks = (idx.shape[0] - 4 * ROOM - own) // 3
    all_tokens = ep_count * tok.shape[0]
    group = picks // slots
    depth = group * chunk
    dma = pltpu.SemaphoreType.DMA
    any_spec = pl.BlockSpec(memory_space=pl.ANY)
    bf16, f32 = jnp.bfloat16, jnp.float32
    return pl.pallas_call(
        functools.partial(stream_kernel, levels, cap, hop, ahead),
        out_shape=[jax.ShapeDtypeStruct((picks, half, width), bf16)] * 3
        + [jax.ShapeDtypeStruct((group, all_tokens, half), bf16)],
        in_specs=[pl.BlockSpec(memory_space=pltpu.SMEM)] + [any_spec] * 5,
        out_specs=[any_spec] * 3 + [pl.BlockSpec(memory_space=pltpu.VMEM)],
        scratch_shapes=[
            [pltpu.VMEM((own, chunk, span), bf16)] * mine_slots,
            [pltpu.VMEM((2 * own + cap, chunk, span), bf16)] * buffers,
            [pltpu.VMEM((2 * own + cap, chunk, span), bf16)] * buffers,
            [pltpu.VMEM((cap, chunk, span), bf16)] * cross_slots,
            pltpu.VMEM((2, cap, chunk, span), bf16),
            pltpu.VMEM((2, cap, chunk, span), bf16),
            pltpu.VMEM((2, cap, chunk, span), bf16),
            pltpu.VMEM((stages, picks, chunk, span), bf16),
            pltpu.VMEM((all_tokens, tok.shape[1]), bf16),
            pltpu.VMEM((all_tokens, mix.shape[2]), f32),
            pltpu.VMEM((2, slots, all_tokens, width), f32),
            pltpu.VMEM((slots, width, all_tokens), bf16),
            pltpu.VMEM((group, depth, all_tokens), f32),
            dma((mine_slots,)),
            dma((2,)),
            dma((buffers,)),
            dma((2,)),
            dma((buffers,)),
            dma((2,)),
            dma((cross_slots,)),
            dma((stages,)),
            dma((ep_count,)),
            dma((ep_count,)),
            dma((ep_count,)),
            dma((ep_count,)),
            dma((2,)),
            pltpu.SemaphoreType.REGULAR,
            pltpu.SemaphoreType.REGULAR,
            pltpu.SemaphoreType.REGULAR,
        ],
        compiler_params=pltpu.CompilerParams(
            collective_id=collective, has_side_effects=True, vmem_limit_bytes=56 * 2**20
        ),
    )(idx, tok, mix, *trains)


def choose(column, slot):
    mixed = column * 40503 + slot * 30011 + 977
    for shift, factor in ((7, 24593), (9, 12289), (5, 6151)):
        mixed = (mixed ^ (mixed >> shift)) & 65535
        mixed = (mixed * factor) & 1048575
    draw = (mixed >> 6) & 255
    return jnp.where(column == 0, 0, jnp.where(draw < 70, 1, jnp.where(draw < 84, 2, 0)))


def routing(train_map, serve_place, ep_index, ep_count, local, parts):
    slots = train_map.shape[0]
    levels = ep_count // 2
    layer = 2 * local
    held = jnp.arange(slots, dtype=jnp.int32)
    level, owner = held // layer, held // local
    side = owner % 2
    floors = jnp.arange(levels, dtype=jnp.int32)
    wanted = serve_place.reshape(ep_count, local)
    need = jnp.any(wanted[:, :, None] == (train_map // parts)[None, None, :], axis=1)
    pairs = need.reshape(levels, 2, slots)
    need_level = jnp.any(pairs, axis=1)
    higher = floors[None, :, None] > floors[:, None, None]
    lower = floors[None, :, None] < floors[:, None, None]
    up = jnp.any(higher & need_level[None], axis=1) & (level[None, :] <= floors[:, None])
    down = jnp.any(lower & need_level[None], axis=1) & (level[None, :] >= floors[:, None])
    here = level[None, :] == floors[:, None]

    def cost(a):
        along = jnp.concatenate([up, down], axis=0)
        away = here & (side[None, :] != a)
        leave = pairs[:, 1 - a] & ~away
        crossing = [leave, away] if a == 0 else [away, leave]
        columns = [along, jnp.zeros_like(along)]
        return jnp.concatenate((columns if a == 0 else columns[::-1]) + crossing, axis=0)

    cost_0, cost_1 = cost(0).astype(jnp.int32), cost(1).astype(jnp.int32)
    number = jnp.arange(CHOICES, dtype=jnp.int32)
    kind = choose(number[:, None], held[None, :])
    in_1 = jnp.where(kind == 0, 1, jnp.where(kind == 1, 2 * side, 2 - 2 * side))
    base = 2 * jnp.sum(cost_0, axis=1)
    change = lax.dot_general(
        in_1.astype(jnp.bfloat16), (cost_1 - cost_0).astype(jnp.bfloat16),
        (((1,), (1,)), ((), ())), preferred_element_type=jnp.float32,
    ).astype(jnp.int32)
    worst = jnp.max(base[None, :] + change, axis=1)
    best = jnp.min(worst * CHOICES + number)
    needed, number = best // CHOICES, best % CHOICES
    kind = choose(number, held)
    in_1 = jnp.where(kind == 0, 1, jnp.where(kind == 1, 2 * side, 2 - 2 * side))

    halves = jnp.arange(2, dtype=jnp.int32)

    def twice(array):
        return jnp.broadcast_to(array[:, None], (slots, 2)).reshape(-1)

    column = jnp.where(
        in_1[:, None] == 1, halves[None, :], (in_1 // 2)[:, None]
    ).reshape(-1)
    z, x = ep_index // 2, ep_index % 2
    partner = ep_index + 1 - 2 * x
    own = 2 * local
    entry = jnp.arange(2 * slots, dtype=jnp.int32)
    entry_owner, entry_level = twice(owner), twice(level)
    same_column = column == x

    def row(array, at):
        return lax.dynamic_index_in_dim(array, at, 0, keepdims=False)

    def along(array, at):
        return twice(row(array, at)) & same_column

    is_mine, is_partner = entry_owner == ep_index, entry_owner == partner
    flags = jnp.stack(
        [
            along(up, z),
            along(down, z),
            along(up, jnp.maximum(z - 1, 0)),
            along(down, jnp.minimum(z + 1, levels - 1)),
            is_mine & ~same_column,
            is_partner & same_column,
            twice(row(need, partner)) & same_column & ~is_partner,
            twice(row(need, ep_index)) & ~same_column & ~is_mine,
        ]
    )
    before = (entry[:, None] < entry[None, :]).astype(jnp.bfloat16)
    place = jnp.dot(
        flags.astype(jnp.bfloat16), before, preferred_element_type=jnp.float32
    ).astype(jnp.int32)
    firsts = jnp.sum(flags[4:6].astype(jnp.int32), axis=1)
    where_low = jnp.where(
        is_mine,
        entry - own * ep_index,
        jnp.where(
            entry_level == z,
            jnp.where(same_column, own + place[5], 0),
            jnp.where((entry_level < z) & same_column, 2 * own + place[2], 0),
        ),
    )
    where_high = jnp.where((entry_level > z) & same_column, 2 * own + place[3], 0)
    where_down = jnp.where(entry_level == z, where_low, where_high)
    where_cross = jnp.where(flags[7], firsts[1] + place[7] + 1, 0)

    def listed(flag, at, room, where):
        hit = flag[None, :] & (at[None, :] == jnp.arange(room, dtype=jnp.int32)[:, None])
        return jnp.sum(jnp.where(hit, where[None, :], 0), axis=1)

    mine = (
        row(wanted, ep_index)[:, None] * parts + jnp.arange(parts, dtype=jnp.int32)[None, :]
    ).reshape(-1)
    mine = (mine[:, None] * 2 + halves[None, :]).reshape(-1)
    named = (train_map[:, None] * 2 + halves[None, :]).reshape(-1)
    same = mine[:, None] == named[None, :]

    def picked(where):
        return jnp.sum(jnp.where(same, where[None, :], 0), axis=1)

    crossing = firsts[0] + place[6]
    tables = jnp.concatenate(
        [
            listed(flags[0], place[0], ROOM, where_low),
            listed(flags[1], place[1], ROOM, where_down),
            listed(flags[4], place[4], own, where_low + 1),
            listed(flags[6], crossing, ROOM, where_low),
            listed(flags[6], crossing, ROOM, where_high),
            picked(where_low),
            picked(where_high),
            picked(where_cross),
        ]
    ).astype(jnp.int32)
    return needed, tables


def stream_body(
    tokens, route_ids, route_weights, train_map, serve_place, train_gate, train_up, train_down
):
    ep_count = lax.axis_size("ep")
    tp_count = lax.axis_size("tp")
    ep_index = lax.axis_index("ep")
    slot_count = serve_place.shape[0]
    local, piece_rows, width = train_gate.shape
    parts = slot_count // EXPERTS
    step_count, tok_count, model_width = tokens.shape
    topk_count = route_ids.shape[2]
    rows = step_count * tok_count
    half, chunk = piece_rows // 2, 16
    full = slot_count - 2 * local
    caps = [c for c in CAPS if c < full] + [full]

    slot_iota = jnp.arange(slot_count, dtype=jnp.int32)
    first = ~jnp.any(
        (serve_place[:, None] == serve_place[None, :]) & (slot_iota[None, :] < slot_iota[:, None]),
        axis=1,
    )
    holder = jnp.where(first, serve_place, -1)
    ids = route_ids.reshape(rows, topk_count)
    weights = route_weights.reshape(rows, topk_count)
    mix = jnp.sum(
        jnp.where(ids[:, :, None] == holder[None, None, :], weights[:, :, None], 0.0), axis=1
    )
    mix = mix.reshape(rows, ep_count, local).transpose(1, 0, 2)
    mix = jnp.pad(mix, ((0, 0), (0, 0), (0, 128 - local)))
    ordered = (
        tokens.reshape(rows, 2 * parts, half // chunk, chunk)
        .transpose(0, 2, 1, 3)
        .reshape(rows, model_width)
    )
    needed, idx = routing(train_map, serve_place, ep_index, ep_count, local, parts)
    choice = sum((needed > c).astype(jnp.int32) for c in caps[:-1])
    trains = [t.reshape(2 * local, half, width) for t in (train_gate, train_up, train_down)]

    def run(collective, cap_static):
        def branch(idx, ordered, mix, *trains):
            return tuple(stream(idx, ordered, mix, trains, ep_count, local, cap_static, collective))

        return branch

    raw_gate, raw_up, raw_down, combined = lax.switch(
        choice, [run(k, c) for k, c in enumerate(caps)], idx, ordered, mix, *trains
    )
    raw_gate, raw_up, raw_down = (
        o.reshape(local, model_width, width) for o in (raw_gate, raw_up, raw_down)
    )
    blocks = 2 * parts // tp_count
    spread = lax.all_to_all(combined, "tp", split_axis=0, concat_axis=0, tiled=True)
    serve_gate, serve_up = settle(raw_gate), settle(raw_up)
    spread, serve_gate, serve_up = lax.optimization_barrier((spread, serve_gate, serve_up))
    spread = spread.reshape(tp_count, blocks, ep_count, rows, half).astype(jnp.float32)
    summed = jnp.sum(spread, axis=0).astype(jnp.bfloat16).transpose(1, 0, 2, 3)
    returned = lax.all_to_all(summed, "ep", split_axis=0, concat_axis=0, tiled=True)
    serve_down = settle(raw_down)
    returned, serve_down = lax.optimization_barrier((returned, serve_down))
    moe_out = jnp.sum(returned.astype(jnp.float32), axis=0).astype(jnp.bfloat16)
    moe_out = moe_out.transpose(1, 0, 2).reshape(
        step_count, tok_count, model_width // tp_count
    )
    return (serve_gate, serve_up, serve_down, moe_out)


def settle_kernel(source, target):
    target[...] = source[...]


def settle(source):
    slots, rows, width = source.shape
    spec = pl.BlockSpec((1, rows, width), lambda i: (i, 0, 0))
    return pl.pallas_call(
        settle_kernel,
        grid=(slots,),
        out_shape=jax.ShapeDtypeStruct(source.shape, source.dtype),
        in_specs=[spec],
        out_specs=spec,
        cost_estimate=pl.CostEstimate(
            flops=0, bytes_accessed=4 * slots * rows * width, transcendentals=0
        ),
    )(source)


def solution(mesh):
    in_specs = (
        P(None, "ep", None),
        P(None, "ep", None),
        P(None, "ep", None),
        P(),
        P(),
        P("ep", None, "tp"),
        P("ep", None, "tp"),
        P("ep", None, "tp"),
    )
    out_specs = (P("ep", None, "tp"), P("ep", None, "tp"), P("ep", None, "tp"), P(None, "ep", "tp"))
    chosen = stream_body if mesh.shape["ep"] <= 8 else body
    return jax.shard_map(chosen, mesh=mesh, in_specs=in_specs, out_specs=out_specs, check_vma=False)
```

```python
import functools

import jax
import jax.numpy as jnp
from jax import lax
from jax.experimental import pallas as pl
from jax.experimental.pallas import tpu as pltpu
from jax.sharding import PartitionSpec as P

EXPERTS = 16
MOST = 10
MESH = pl.DeviceIdType.MESH
CAPS = (31, 32, 33, 34, 36, 38, 41)
ROOM = 48
CHOICES = 2048
SPAN = 128
HOP = 2
AHEAD = 2


def relay_kernel(
    pairs, chunk_rows, buffers, idx_ref, t0, t1, t2, o0, o1, o2, held, whole, own, other,
    local_sem, first_send, first_recv, line_send, line_recv,
    own_sem, other_send, other_recv, stage_sem, credit_x, credit_up, credit_down,
):
    trains, outs = (t0, t1, t2), (o0, o1, o2)
    me = lax.axis_index("ep")
    z, x = lax.div(me, 2), lax.rem(me, 2)
    partner = me + 1 - 2 * x
    above, below = me + 2, me - 2
    local = t0.shape[0]
    half = t0.shape[1] // 2
    steps = half // chunk_rows
    total = len(trains) * steps
    layer = 2 * local
    picks = own.shape[1]
    recv_slots = other_recv.shape[0]
    has_up, has_down = z < pairs - 1, z > 0

    barrier = pltpu.get_barrier_semaphore()
    pl.semaphore_signal(barrier, inc=1, device_id={"ep": partner}, device_id_type=MESH)

    @pl.when(has_up)
    def _():
        pl.semaphore_signal(barrier, inc=1, device_id={"ep": above}, device_id_type=MESH)

    @pl.when(has_down)
    def _():
        pl.semaphore_signal(barrier, inc=1, device_id={"ep": below}, device_id_type=MESH)

    pl.semaphore_wait(barrier, 1 + jnp.where(has_up, 1, 0) + jnp.where(has_down, 1, 0))

    def rows_of(side, step):
        return pl.ds(pl.multiple_of(side * half + step * chunk_rows, chunk_rows), chunk_rows)

    def mine(slot):
        return held.at[slot, pl.ds(me * local, local)]

    def region(slot, level):
        return held.at[slot, pl.ds(level * layer, layer)]

    def load_copy(train, step, slot):
        return pltpu.make_async_copy(
            train.at[:, rows_of(x, step), :], mine(slot), local_sem.at[slot]
        )

    def first_copy(train, step, slot):
        return pltpu.make_async_remote_copy(
            src_ref=train.at[:, rows_of(1 - x, step), :],
            dst_ref=mine(slot),
            send_sem=first_send.at[slot],
            recv_sem=first_recv.at[slot],
            device_id={"ep": partner},
            device_id_type=MESH,
        )

    def up_copy(slot, level):
        return pltpu.make_async_remote_copy(
            src_ref=region(slot, level),
            dst_ref=region(slot, level),
            send_sem=line_send.at[slot, level],
            recv_sem=line_recv.at[slot, level],
            device_id={"ep": above},
            device_id_type=MESH,
        )

    def down_copy(slot, level):
        return pltpu.make_async_remote_copy(
            src_ref=region(slot, level),
            dst_ref=region(slot, level),
            send_sem=line_send.at[slot, level + 1],
            recv_sem=line_recv.at[slot, level],
            device_id={"ep": below},
            device_id_type=MESH,
        )

    def own_copy(out, step, stage):
        return pltpu.make_async_copy(
            own.at[stage], out.at[:, rows_of(x, step), :], own_sem.at[stage]
        )

    def other_copy(out, step, stage, recv_slot):
        return pltpu.make_async_remote_copy(
            src_ref=other.at[stage],
            dst_ref=out.at[:, rows_of(x, step), :],
            send_sem=other_send.at[stage],
            recv_sem=other_recv.at[recv_slot],
            device_id={"ep": partner},
            device_id_type=MESH,
        )

    def stage_start(n):
        slot = lax.rem(n, buffers)

        @pl.when(n >= buffers)
        def _():
            pl.semaphore_wait(credit_x, 1)

        for a in range(len(trains)):

            @pl.when((n >= a * steps) & (n < (a + 1) * steps))
            def _():
                first_copy(trains[a], n - a * steps, slot).start()
                load_copy(trains[a], n - a * steps, slot).start()

    def stage_send(n):
        slot = lax.rem(n, buffers)
        load_copy(t0, 0, slot).wait()
        first_copy(t0, 0, slot).wait()

        @pl.when(has_up)
        def _():
            @pl.when(n >= buffers)
            def _():
                pl.semaphore_wait(credit_up, 1)

            up_copy(slot, z).start()

        @pl.when(has_down)
        def _():
            @pl.when(n >= buffers)
            def _():
                pl.semaphore_wait(credit_down, 1)

            down_copy(slot, z).start()

    def stage_forward(n, distance):
        slot = lax.rem(n, buffers)

        @pl.when(z - distance >= 0)
        def _():
            up_copy(slot, z - distance).wait_recv()

            @pl.when(has_up)
            def _():
                up_copy(slot, z - distance).start()

        @pl.when(z + distance < pairs)
        def _():
            down_copy(slot, z + distance).wait_recv()

            @pl.when(has_down)
            def _():
                down_copy(slot, z + distance).start()

    def stage_finish(n):
        slot = lax.rem(n, buffers)
        stage = lax.rem(n, 2)
        taken = pltpu.make_async_copy(held.at[slot], whole, stage_sem)
        taken.start()

        def drain_up(level, carry):
            up_copy(slot, level).wait_send()
            return carry

        def drain_down(level, carry):
            down_copy(slot, level).wait_send()
            return carry

        @pl.when(has_up)
        def _():
            lax.fori_loop(0, z + 1, drain_up, 0)

        @pl.when(has_down)
        def _():
            lax.fori_loop(z, pairs, drain_down, 0)

        taken.wait()

        @pl.when(n < total - buffers)
        def _():
            pl.semaphore_signal(credit_x, inc=1, device_id={"ep": partner}, device_id_type=MESH)

            @pl.when(has_up)
            def _():
                pl.semaphore_signal(
                    credit_down, inc=1, device_id={"ep": above}, device_id_type=MESH
                )

            @pl.when(has_down)
            def _():
                pl.semaphore_signal(
                    credit_up, inc=1, device_id={"ep": below}, device_id_type=MESH
                )

        @pl.when(n >= 2)
        def _():
            own_copy(o0, 0, stage).wait()
            other_copy(o0, 0, stage, 0).wait_send()

        @pl.when(n >= 1)
        def _():
            other_copy(o0, 0, stage, lax.rem(n - 1, recv_slots)).wait_recv()

        def pick(s, carry):
            other[stage, s] = whole[idx_ref[picks + s]]
            own[stage, s] = whole[idx_ref[s]]
            return carry

        lax.fori_loop(0, picks, pick, 0)
        for a in range(len(trains)):

            @pl.when((n >= a * steps) & (n < (a + 1) * steps))
            def _():
                other_copy(outs[a], n - a * steps, stage, lax.rem(n, recv_slots)).start()
                own_copy(outs[a], n - a * steps, stage).start()

    def iteration(i, carry):
        @pl.when(i < total)
        def _():
            stage_start(i)

        @pl.when((i >= 1) & (i - 1 < total))
        def _():
            stage_send(i - 1)

        def hop(distance, inner):
            n = i - 1 - distance

            @pl.when((n >= 0) & (n < total))
            def _():
                stage_forward(n, distance)

            return inner

        lax.fori_loop(1, pairs, hop, 0)

        @pl.when(i >= pairs)
        def _():
            stage_finish(i - pairs)

        return carry

    lax.fori_loop(0, total + pairs, iteration, 0)
    for n in range(max(total - 2, 0), total):
        own_copy(o0, 0, n % 2).wait()
        other_copy(o0, 0, n % 2, 0).wait_send()
    other_copy(o0, 0, 0, (total - 1) % recv_slots).wait_recv()


def relay(idx, trains, ep_count, part_count):
    local, piece_rows, width = trains[0].shape
    pairs = ep_count // 2
    slots = ep_count * local
    buffers = pairs + 3
    chunk_rows = 32
    while chunk_rows > 16 and buffers * slots * chunk_rows * width * 2 > 24 * 2**20:
        chunk_rows //= 2
    picks = local * part_count
    dma = pltpu.SemaphoreType.DMA
    any_spec = pl.BlockSpec(memory_space=pl.ANY)
    return pl.pallas_call(
        functools.partial(relay_kernel, pairs, chunk_rows, buffers),
        out_shape=[jax.ShapeDtypeStruct((picks, piece_rows, width), jnp.bfloat16)] * 3,
        in_specs=[pl.BlockSpec(memory_space=pltpu.SMEM)] + [any_spec] * 3,
        out_specs=[any_spec] * 3,
        scratch_shapes=[
            pltpu.VMEM((buffers, slots, chunk_rows, width), jnp.bfloat16),
            pltpu.VMEM((slots, chunk_rows, width), jnp.bfloat16),
            pltpu.VMEM((2, picks, chunk_rows, width), jnp.bfloat16),
            pltpu.VMEM((2, picks, chunk_rows, width), jnp.bfloat16),
            dma((buffers,)),
            dma((buffers,)),
            dma((buffers,)),
            dma((buffers, pairs + 1)),
            dma((buffers, pairs)),
            dma((2,)),
            dma((2,)),
            dma((buffers + 2,)),
            dma,
            pltpu.SemaphoreType.REGULAR,
            pltpu.SemaphoreType.REGULAR,
            pltpu.SemaphoreType.REGULAR,
        ],
        compiler_params=pltpu.CompilerParams(
            collective_id=0, has_side_effects=True, vmem_limit_bytes=56 * 2**20
        ),
    )(idx, *trains)


def body(
    tokens, route_ids, route_weights, train_map, serve_place, train_gate, train_up, train_down
):
    ep_count = lax.axis_size("ep")
    tp_count = lax.axis_size("tp")
    ep_index = lax.axis_index("ep")
    slot_count = serve_place.shape[0]
    local_slots, piece_rows, quarter_width = train_gate.shape
    part_count = slot_count // EXPERTS
    slot_iota = jnp.arange(slot_count, dtype=jnp.int32)
    inverse = jnp.sum(
        jnp.where(train_map[:, None] == slot_iota[None, :], slot_iota[:, None], 0), axis=0
    )
    wanted = (
        serve_place[:, None] * part_count + jnp.arange(part_count, dtype=jnp.int32)[None, :]
    ).reshape(-1)
    source_slot = jnp.sum(
        jnp.where(wanted[:, None] == slot_iota[None, :], inverse[None, :], 0), axis=1
    ).reshape(ep_count, local_slots * part_count)
    partner = ep_index + 1 - 2 * (ep_index % 2)
    idx = jnp.concatenate(
        [
            lax.dynamic_index_in_dim(source_slot, ep_index, 0, keepdims=False),
            lax.dynamic_index_in_dim(source_slot, partner, 0, keepdims=False),
        ]
    ).astype(jnp.int32)
    model_rows = part_count * piece_rows
    raw_gate, raw_up, raw_down = (
        o.reshape(local_slots, model_rows, quarter_width)
        for o in relay(idx, (train_gate, train_up, train_down), ep_count, part_count)
    )

    step_count, tok_count, model_width = tokens.shape
    topk_count = route_ids.shape[2]
    capacity = (MOST + 1) // 2
    depth = capacity * step_count
    peer_rows = depth * local_slots
    all_tokens = step_count * tok_count
    same_slot = serve_place[:, None] == serve_place[None, :]
    replica_rank = jnp.sum(same_slot & (slot_iota[None, :] < slot_iota[:, None]), axis=1)
    pair_count = tok_count * topk_count
    pair_iota = jnp.arange(pair_count, dtype=jnp.int32)

    def rows(ids, decode_step):
        pair_experts = ids.reshape(pair_count)
        holders = serve_place[None, :] == pair_experts[:, None]
        replica_count = jnp.sum(holders, axis=1)
        earlier_pairs = (pair_experts[:, None] == pair_experts[None, :]) & (
            pair_iota[None, :] < pair_iota[:, None]
        )
        seen = jnp.sum(earlier_pairs, axis=1)
        target = (seen + ep_index) % replica_count
        position = seen // replica_count
        chosen = holders & (replica_rank[None, :] == target[:, None])
        dest_slot = jnp.sum(jnp.where(chosen, slot_iota[None, :], 0), axis=1)
        return (
            dest_slot // local_slots * peer_rows
            + (decode_step * capacity + position) * local_slots
            + dest_slot % local_slots
        )

    row_index = jax.vmap(rows)(route_ids, jnp.arange(step_count, dtype=jnp.int32))
    row_index = row_index.reshape(1, all_tokens, topk_count)
    buffer_iota = jnp.arange(ep_count * peer_rows, dtype=jnp.int32)
    placing = row_index == buffer_iota[:, None, None]
    mixing = jnp.sum(
        jnp.where(placing, route_weights.reshape(1, all_tokens, topk_count), 0.0), axis=2
    )
    send_rows = jnp.dot(
        jnp.any(placing, axis=2).astype(jnp.bfloat16),
        tokens.reshape(all_tokens, model_width),
        preferred_element_type=jnp.float32,
    ).astype(jnp.bfloat16)
    received = lax.all_to_all(
        send_rows.reshape(ep_count, depth, local_slots, model_width),
        "ep", split_axis=0, concat_axis=0, tiled=True,
    ).reshape(ep_count * depth, local_slots, model_width)
    mix = lax.all_to_all(
        mixing.reshape(ep_count, peer_rows, all_tokens),
        "ep", split_axis=0, concat_axis=0, tiled=True,
    )
    gate_act = jnp.einsum("mld,ldf->lmf", received, raw_gate, preferred_element_type=jnp.float32)
    up_act = jnp.einsum("mld,ldf->lmf", received, raw_up, preferred_element_type=jnp.float32)
    hidden = (jax.nn.silu(gate_act) * up_act).astype(jnp.bfloat16)
    partial_value = jnp.einsum(
        "lmf,ldf->lmd", hidden, raw_down, preferred_element_type=jnp.float32
    ).astype(jnp.bfloat16)
    mix = mix.reshape(ep_count, depth, local_slots, all_tokens)
    mix_high = mix.astype(jnp.bfloat16)
    mix_low = (mix - mix_high.astype(jnp.float32)).astype(jnp.bfloat16)
    rows_out = partial_value.reshape(local_slots, ep_count, depth, model_width)

    def combine(part):
        return jnp.einsum("pclt,lpcd->ptd", part, rows_out, preferred_element_type=jnp.float32)

    combined = (combine(mix_high) + combine(mix_low)).astype(jnp.bfloat16)
    combined = lax.optimization_barrier(combined)
    summed = lax.psum_scatter(combined, "tp", scatter_dimension=2, tiled=True)
    raw_gate, raw_up, raw_down, _ = lax.optimization_barrier(
        (raw_gate, raw_up, raw_down, combined)
    )
    serve_gate, serve_up, serve_down = (settle(o) for o in (raw_gate, raw_up, raw_down))
    summed, serve_gate, serve_up = lax.optimization_barrier((summed, serve_gate, serve_up))
    returned = lax.all_to_all(summed, "ep", split_axis=0, concat_axis=0, tiled=True)
    moe_out = jnp.sum(returned.astype(jnp.float32), axis=0).astype(jnp.bfloat16)
    moe_out = moe_out.reshape(step_count, tok_count, model_width // tp_count)
    return (serve_gate, serve_up, serve_down, moe_out)


def stream_kernel(
    levels, cap, hop, ahead, idx_ref, tok_ref, mix_ref, t0, t1, t2, o0, o1, o2, part_ref,
    mines, lows, highs, crosses, ups, downs, across, stage, tokens, lhs, mix, acc, hid, flipped,
    mine_sem, up_send, up_recv, down_send, down_recv, across_send, cross_recv, out_sem,
    tok_send, tok_recv, mix_send, mix_recv, here_sem, credit_up, credit_down, credit_cross,
):
    trains, outs = (t0, t1, t2), (o0, o1, o2)
    me = lax.axis_index("ep")
    ep_count = 2 * levels
    z, x = lax.div(me, 2), lax.rem(me, 2)
    partner = me + 1 - 2 * x
    above, below = me + 2, me - 2
    own, half, width = t0.shape
    chunk, span = ups.shape[2], ups.shape[3]
    splits = width // span
    steps = half // chunk
    per_array = steps * splits
    total = len(trains) * per_array
    picks = stage.shape[1]
    slots = hid.shape[0]
    depth = picks // slots * chunk
    layer = 2 * own
    buffers, mine_slots = len(lows), len(mines)
    cross_slots, stages = len(crosses), stage.shape[0]
    senders = ups.shape[0]
    group = depth // chunk
    tok_rows = tok_ref.shape[0]
    up_at, down_at, first_at = 0, ROOM, 2 * ROOM
    cross_at = first_at + own
    pick_at = cross_at + 2 * ROOM
    has_up, has_down = z < levels - 1, z > 0
    travel = levels * hop

    def to(device):
        return {"device_id": {"ep": device}, "device_id_type": MESH}

    barrier = pltpu.get_barrier_semaphore()

    def greet(k, carry):
        pl.semaphore_signal(barrier, inc=1, **to(lax.rem(me + k, ep_count)))
        return carry

    lax.fori_loop(1, ep_count, greet, 0)
    pl.semaphore_wait(barrier, ep_count - 1)

    def my_rows(ref):
        return ref.at[pl.ds(pl.multiple_of(me * tok_rows, 16), tok_rows)]

    def tok_copy(k):
        return pltpu.make_async_remote_copy(
            src_ref=tok_ref,
            dst_ref=my_rows(tokens),
            send_sem=tok_send.at[k],
            recv_sem=tok_recv.at[k],
            **to(lax.rem(me + k, ep_count)),
        )

    def mix_copy(k):
        peer = lax.rem(me + k, ep_count)
        return pltpu.make_async_remote_copy(
            src_ref=mix_ref.at[peer],
            dst_ref=my_rows(mix),
            send_sem=mix_send.at[k],
            recv_sem=mix_recv.at[k],
            **to(peer),
        )

    def tok_here():
        return pltpu.make_async_copy(tok_ref, my_rows(tokens), here_sem.at[0])

    def mix_here():
        return pltpu.make_async_copy(mix_ref.at[me], my_rows(mix), here_sem.at[1])

    def part_of(array, at):
        step, column = lax.div(at, splits), lax.rem(at, splits)
        rows = pl.ds(pl.multiple_of(step * chunk, chunk), chunk)
        return array.at[:, rows, pl.ds(pl.multiple_of(column * span, span), span)]

    def mine_copy(train, at, slot):
        return pltpu.make_async_copy(part_of(train, at), mines[slot], mine_sem.at[slot])

    def up_copy(side, slot):
        return pltpu.make_async_remote_copy(
            src_ref=ups.at[side],
            dst_ref=lows[slot].at[pl.ds(layer, cap)],
            send_sem=up_send.at[side],
            recv_sem=up_recv.at[slot],
            **to(above),
        )

    def down_copy(side, slot):
        return pltpu.make_async_remote_copy(
            src_ref=downs.at[side],
            dst_ref=highs[slot].at[pl.ds(layer, cap)],
            send_sem=down_send.at[side],
            recv_sem=down_recv.at[slot],
            **to(below),
        )

    def across_copy(side, slot):
        return pltpu.make_async_remote_copy(
            src_ref=across.at[side],
            dst_ref=crosses[slot],
            send_sem=across_send.at[side],
            recv_sem=cross_recv.at[slot],
            **to(partner),
        )

    def out_copy(out, at, place):
        return pltpu.make_async_copy(stage.at[place], part_of(out, at), out_sem.at[place])

    def each_array(n, action):
        for a in range(len(trains)):

            @pl.when((n >= a * per_array) & (n < (a + 1) * per_array))
            def _():
                action(a, n - a * per_array)

    def each_slot(n, count, action):
        for b in range(count):

            @pl.when(lax.rem(n, count) == b)
            def _():
                action(b)

    def gather(start, stop, put, take):
        wide = 4

        def several(g, carry):
            for k in range(wide):
                put(start + g * wide + k, take(start + g * wide + k))
            return carry

        full = (stop - start) // wide
        lax.fori_loop(0, full, several, 0)
        for j in range(start + full * wide, stop):
            put(j, take(j))

    def load(n):
        def go(slot, a, at):
            mine_copy(trains[a], at, slot).start()

        each_slot(n, mine_slots, lambda b: each_array(n, functools.partial(go, b)))

    def either(slot, j, far):
        high = idx_ref[j + far]
        return jnp.where(high > 0, highs[slot][high], lows[slot][idx_ref[j]])

    def send_across(m):
        side = lax.rem(m, senders)
        n = m - travel

        @pl.when(m >= senders)
        def _():
            across_copy(side, 0).wait_send()

        def put(j, value):
            across[side, j] = value

        @pl.when(m < total)
        def _():
            def go(slot):
                mine_copy(t0, 0, slot).wait()
                gather(0, own, put, lambda j: mines[slot][jnp.maximum(idx_ref[first_at + j] - 1, 0)])

            each_slot(m, mine_slots, go)

        @pl.when(n >= 0)
        def _():
            def mixed(slot, j):
                is_first = idx_ref[first_at + j] > 0
                return jnp.where(is_first, across[side, j], either(slot, cross_at + j, ROOM))

            def go(slot):
                gather(0, own, put, functools.partial(mixed, slot))
                gather(own, cap, put, lambda j: either(slot, cross_at + j, ROOM))

            each_slot(n, buffers, go)

        @pl.when(m >= cross_slots)
        def _():
            pl.semaphore_wait(credit_cross, 1)

        each_slot(m, cross_slots, lambda b: across_copy(side, b).start())

    def take_first(n):
        def from_mine(slot, source):
            def both(j, value):
                lows[slot][j] = value
                highs[slot][j] = value

            gather(0, own, both, lambda j: mines[source][j])

        def from_partner(slot, source):
            def both(j, value):
                lows[slot][own + j] = value
                highs[slot][own + j] = value

            gather(0, own, both, lambda j: crosses[source][j])

        def go(slot):
            each_slot(n, mine_slots, functools.partial(from_mine, slot))
            each_slot(n, cross_slots, functools.partial(from_partner, slot))

        each_slot(n, buffers, go)

    def send_up(n):
        side = lax.rem(n, senders)

        @pl.when(has_up & (n >= senders))
        def _():
            up_copy(side, 0).wait_send()

        def put(j, value):
            ups[side, j] = value

        def go(slot):
            @pl.when(has_down)
            def _():
                up_copy(side, slot).wait_recv()

            @pl.when(has_up)
            def _():
                gather(0, cap, put, lambda j: lows[slot][idx_ref[up_at + j]])

                @pl.when(n >= buffers)
                def _():
                    pl.semaphore_wait(credit_up, 1)

                up_copy(side, slot).start()

        each_slot(n, buffers, go)

    def send_down(n):
        side = lax.rem(n, senders)

        @pl.when(has_down & (n >= senders))
        def _():
            down_copy(side, 0).wait_send()

        def put(j, value):
            downs[side, j] = value

        def go(slot):
            @pl.when(has_up)
            def _():
                down_copy(side, slot).wait_recv()

            @pl.when(has_down)
            def _():
                gather(0, cap, put, lambda j: highs[slot][idx_ref[down_at + j]])

                @pl.when(n >= buffers)
                def _():
                    pl.semaphore_wait(credit_down, 1)

                down_copy(side, slot).start()

        each_slot(n, buffers, go)

    def collect(n):
        place = lax.rem(n, stages)

        @pl.when(n >= stages)
        def _():
            out_copy(o0, 0, place).wait()

        def keep(j, value):
            stage[place, j] = value

        def go(slot):
            gather(0, picks, keep, lambda j: either(slot, pick_at + j, picks))

        each_slot(n, buffers, go)

        @pl.when(n < total - buffers)
        def _():
            @pl.when(has_up)
            def _():
                pl.semaphore_signal(credit_down, inc=1, **to(above))

            @pl.when(has_down)
            def _():
                pl.semaphore_signal(credit_up, inc=1, **to(below))

    def slot_weights(place, s):
        return stage[place, pl.ds(s * (picks // slots), picks // slots)].reshape(depth, span)

    def finish(n):
        place = lax.rem(n, stages)
        at = lax.rem(n, per_array)
        step, column = lax.div(at, splits), lax.rem(at, splits)
        columns = pl.ds(pl.multiple_of(column * span, span), span)

        def keep(j, value):
            stage[place, j] = value

        def other(slot):
            def take(j):
                there = idx_ref[pick_at + 2 * picks + j]
                return jnp.where(
                    there > 0, crosses[slot][jnp.maximum(there - 1, 0)], stage[place, j]
                )

            gather(0, picks, keep, take)

        each_slot(n + travel, cross_slots, other)
        each_array(n, lambda a, where: out_copy(outs[a], where, place).start())

        @pl.when(n == 0)
        def _():
            tok_here().wait()
            mix_here().wait()

            def arrive(k, carry):
                tok_copy(k).wait()
                mix_copy(k).wait()
                return carry

            lax.fori_loop(1, ep_count, arrive, 0)

        @pl.when(n < 2 * per_array)
        def _():
            which = lax.div(n, per_array)

            @pl.when(column == 0)
            def _():
                base = lax.div(step, group) * depth
                wanted = lax.broadcasted_iota(jnp.int32, (depth, depth), 1)
                held = lax.broadcasted_iota(jnp.int32, (depth, depth), 0)
                found = lax.rem(step, group) * chunk + lax.rem(wanted, chunk)
                chosen = jnp.zeros(lhs.shape, jnp.float32)
                for k in range(group):
                    hit = (held == found) & (lax.div(wanted, chunk) == k)
                    chosen += jnp.dot(
                        tokens[:, pl.ds(pl.multiple_of(k * half + base, depth), depth)],
                        jnp.where(hit, 1.0, 0.0).astype(jnp.bfloat16),
                        preferred_element_type=jnp.float32,
                    )
                lhs[...] = chosen.astype(jnp.bfloat16)

            def add(s, carry):
                acc[which, s, :, columns] += jnp.dot(
                    lhs[...], slot_weights(place, s), preferred_element_type=jnp.float32
                )
                return carry

            lax.fori_loop(0, slots, add, 0)

        @pl.when(n == 2 * per_array)
        def _():
            block = 128
            blocks = tokens.shape[0] // block
            lane = lax.broadcasted_iota(jnp.int32, (block, mix.shape[1]), 1)

            def act(i, carry):
                s, b = lax.div(i, blocks), lax.rem(i, blocks)
                rows = pl.ds(pl.multiple_of(b * block, block), block)
                scale = jnp.sum(jnp.where(lane == s, mix[rows, :], 0.0), axis=1, keepdims=True)
                gate = acc[0, s, rows, :]
                value = gate / (1.0 + jnp.exp(-gate)) * acc[1, s, rows, :] * scale
                hid[s, :, rows] = value.T.astype(jnp.bfloat16)
                return carry

            lax.fori_loop(0, slots * blocks, act, 0)

        @pl.when(n >= 2 * per_array)
        def _():
            def add(s, carry):
                return carry + jnp.dot(
                    slot_weights(place, s), hid[s, columns, :],
                    preferred_element_type=jnp.float32,
                )

            mixed = lax.fori_loop(0, slots, add, jnp.zeros((depth, tokens.shape[0]), jnp.float32))
            inner = lax.rem(step, group)
            rows = pl.ds(pl.multiple_of(inner * chunk, chunk), chunk)
            for k in range(group):
                piece = mixed[k * chunk : (k + 1) * chunk]
                before = jnp.where(column == 0, jnp.zeros_like(piece), flipped[k, rows, :])
                flipped[k, rows, :] = before + piece

            @pl.when((inner == group - 1) & (column == splits - 1))
            def _():
                for k in range(group):
                    place_at = pl.multiple_of(lax.div(step, group) * depth, depth)
                    part_ref[k, :, pl.ds(place_at, depth)] = flipped[k].T.astype(jnp.bfloat16)

    def spread(k, carry):
        tok_copy(k).start()
        mix_copy(k).start()
        return carry

    def clear(s, carry):
        for a in range(2):
            acc[a, s] = jnp.zeros(acc.shape[2:], jnp.float32)
        return carry

    def within(n):
        return (n >= 0) & (n < total)

    def iteration(i, carry):
        @pl.when(i < total)
        def _():
            load(i)

        @pl.when(i == 0)
        def _():
            lax.fori_loop(1, ep_count, spread, 0)
            tok_here().start()
            mix_here().start()
            lax.fori_loop(0, slots, clear, 0)

        m = i - ahead - hop
        arrived = (m >= 0) & (m < total + travel)

        @pl.when(arrived)
        def _():
            each_slot(m, cross_slots, lambda b: across_copy(0, b).wait_recv())

        @pl.when(within(m))
        def _():
            take_first(m)

        n_up = m - z * hop

        @pl.when(within(n_up))
        def _():
            send_up(n_up)

        n_down = m - (levels - 1 - z) * hop

        @pl.when(within(n_down))
        def _():
            send_down(n_down)

        @pl.when((i >= ahead) & (i - ahead < total + travel))
        def _():
            send_across(i - ahead)

        @pl.when(within(i - ahead - travel))
        def _():
            collect(i - ahead - travel)

        @pl.when(within(m - travel))
        def _():
            finish(m - travel)

        @pl.when(arrived & (m < total + travel - cross_slots))
        def _():
            pl.semaphore_signal(credit_cross, inc=1, **to(partner))

        return carry

    lax.fori_loop(0, total + travel + ahead + hop, iteration, 0)
    for n in range(senders):

        @pl.when(has_up)
        def _():
            up_copy(n, 0).wait_send()

        @pl.when(has_down)
        def _():
            down_copy(n, 0).wait_send()

        across_copy(n, 0).wait_send()
    for n in range(stages):
        out_copy(o0, 0, n).wait()


def stream(idx, tok, mix, trains, ep_count, slots, cap, collective):
    own, half, width = trains[0].shape
    levels = ep_count // 2
    chunk, span = 16, SPAN
    hop, ahead = HOP, AHEAD
    buffers = (levels - 1) * hop + 4
    mine_slots = ahead + hop + 1
    cross_slots = hop + 3
    stages, senders = hop + 3, 2
    picks = (idx.shape[0] - 4 * ROOM - own) // 3
    all_tokens = ep_count * tok.shape[0]
    group = picks // slots
    depth = group * chunk
    dma = pltpu.SemaphoreType.DMA
    any_spec = pl.BlockSpec(memory_space=pl.ANY)
    bf16, f32 = jnp.bfloat16, jnp.float32
    return pl.pallas_call(
        functools.partial(stream_kernel, levels, cap, hop, ahead),
        out_shape=[jax.ShapeDtypeStruct((picks, half, width), bf16)] * 3
        + [jax.ShapeDtypeStruct((group, all_tokens, half), bf16)],
        in_specs=[pl.BlockSpec(memory_space=pltpu.SMEM)] + [any_spec] * 5,
        out_specs=[any_spec] * 3 + [pl.BlockSpec(memory_space=pltpu.VMEM)],
        scratch_shapes=[
            [pltpu.VMEM((own, chunk, span), bf16)] * mine_slots,
            [pltpu.VMEM((2 * own + cap, chunk, span), bf16)] * buffers,
            [pltpu.VMEM((2 * own + cap, chunk, span), bf16)] * buffers,
            [pltpu.VMEM((cap, chunk, span), bf16)] * cross_slots,
            pltpu.VMEM((senders, cap, chunk, span), bf16),
            pltpu.VMEM((senders, cap, chunk, span), bf16),
            pltpu.VMEM((senders, cap, chunk, span), bf16),
            pltpu.VMEM((stages, picks, chunk, span), bf16),
            pltpu.VMEM((all_tokens, tok.shape[1]), bf16),
            pltpu.VMEM((all_tokens, depth), bf16),
            pltpu.VMEM((all_tokens, mix.shape[2]), f32),
            pltpu.VMEM((2, slots, all_tokens, width), f32),
            pltpu.VMEM((slots, width, all_tokens), bf16),
            pltpu.VMEM((group, depth, all_tokens), f32),
            dma((mine_slots,)),
            dma((senders,)),
            dma((buffers,)),
            dma((senders,)),
            dma((buffers,)),
            dma((senders,)),
            dma((cross_slots,)),
            dma((stages,)),
            dma((ep_count,)),
            dma((ep_count,)),
            dma((ep_count,)),
            dma((ep_count,)),
            dma((2,)),
            pltpu.SemaphoreType.REGULAR,
            pltpu.SemaphoreType.REGULAR,
            pltpu.SemaphoreType.REGULAR,
        ],
        compiler_params=pltpu.CompilerParams(
            collective_id=collective, has_side_effects=True, vmem_limit_bytes=56 * 2**20
        ),
    )(idx, tok, mix, *trains)


def choose(column, slot):
    mixed = column * 40503 + slot * 30011 + 977
    for shift, factor in ((7, 24593), (9, 12289), (5, 6151)):
        mixed = (mixed ^ (mixed >> shift)) & 65535
        mixed = (mixed * factor) & 1048575
    draw = (mixed >> 6) & 255
    return jnp.where(column == 0, 0, jnp.where(draw < 70, 1, jnp.where(draw < 84, 2, 0)))


def routing(train_map, serve_place, ep_index, ep_count, local, parts):
    slots = train_map.shape[0]
    levels = ep_count // 2
    layer = 2 * local
    held = jnp.arange(slots, dtype=jnp.int32)
    level, owner = held // layer, held // local
    side = owner % 2
    floors = jnp.arange(levels, dtype=jnp.int32)
    wanted = serve_place.reshape(ep_count, local)
    need = jnp.any(wanted[:, :, None] == (train_map // parts)[None, None, :], axis=1)
    pairs = need.reshape(levels, 2, slots)
    need_level = jnp.any(pairs, axis=1)
    higher = floors[None, :, None] > floors[:, None, None]
    lower = floors[None, :, None] < floors[:, None, None]
    up = jnp.any(higher & need_level[None], axis=1) & (level[None, :] <= floors[:, None])
    down = jnp.any(lower & need_level[None], axis=1) & (level[None, :] >= floors[:, None])
    here = level[None, :] == floors[:, None]

    def cost(a):
        along = jnp.concatenate([up, down], axis=0)
        away = here & (side[None, :] != a)
        leave = pairs[:, 1 - a] & ~away
        crossing = [leave, away] if a == 0 else [away, leave]
        columns = [along, jnp.zeros_like(along)]
        return jnp.concatenate((columns if a == 0 else columns[::-1]) + crossing, axis=0)

    cost_0, cost_1 = cost(0).astype(jnp.int32), cost(1).astype(jnp.int32)
    number = jnp.arange(CHOICES, dtype=jnp.int32)
    kind = choose(number[:, None], held[None, :])
    in_1 = jnp.where(kind == 0, 1, jnp.where(kind == 1, 2 * side, 2 - 2 * side))
    base = 2 * jnp.sum(cost_0, axis=1)
    change = lax.dot_general(
        in_1.astype(jnp.bfloat16), (cost_1 - cost_0).astype(jnp.bfloat16),
        (((1,), (1,)), ((), ())), preferred_element_type=jnp.float32,
    ).astype(jnp.int32)
    worst = jnp.max(base[None, :] + change, axis=1)
    best = jnp.min(worst * CHOICES + number)
    needed, number = best // CHOICES, best % CHOICES
    kind = choose(number, held)
    in_1 = jnp.where(kind == 0, 1, jnp.where(kind == 1, 2 * side, 2 - 2 * side))

    halves = jnp.arange(2, dtype=jnp.int32)

    def twice(array):
        return jnp.broadcast_to(array[:, None], (slots, 2)).reshape(-1)

    column = jnp.where(
        in_1[:, None] == 1, halves[None, :], (in_1 // 2)[:, None]
    ).reshape(-1)
    z, x = ep_index // 2, ep_index % 2
    partner = ep_index + 1 - 2 * x
    own = 2 * local
    entry = jnp.arange(2 * slots, dtype=jnp.int32)
    entry_owner, entry_level = twice(owner), twice(level)
    same_column = column == x

    def row(array, at):
        return lax.dynamic_index_in_dim(array, at, 0, keepdims=False)

    def along(array, at):
        return twice(row(array, at)) & same_column

    is_mine, is_partner = entry_owner == ep_index, entry_owner == partner
    flags = jnp.stack(
        [
            along(up, z),
            along(down, z),
            along(up, jnp.maximum(z - 1, 0)),
            along(down, jnp.minimum(z + 1, levels - 1)),
            is_mine & ~same_column,
            is_partner & same_column,
            twice(row(need, partner)) & same_column & ~is_partner,
            twice(row(need, ep_index)) & ~same_column & ~is_mine,
        ]
    )
    before = (entry[:, None] < entry[None, :]).astype(jnp.bfloat16)
    place = jnp.dot(
        flags.astype(jnp.bfloat16), before, preferred_element_type=jnp.float32
    ).astype(jnp.int32)
    firsts = jnp.sum(flags[4:6].astype(jnp.int32), axis=1)
    where_low = jnp.where(
        is_mine,
        entry - own * ep_index,
        jnp.where(
            entry_level == z,
            jnp.where(same_column, own + place[5], 0),
            jnp.where((entry_level < z) & same_column, 2 * own + place[2], 0),
        ),
    )
    where_high = jnp.where((entry_level > z) & same_column, 2 * own + place[3], 0)
    where_down = jnp.where(entry_level == z, where_low, where_high)
    where_cross = jnp.where(flags[7], firsts[1] + place[7] + 1, 0)

    def listed(flag, at, room, where):
        hit = flag[None, :] & (at[None, :] == jnp.arange(room, dtype=jnp.int32)[:, None])
        return jnp.sum(jnp.where(hit, where[None, :], 0), axis=1)

    mine = (
        row(wanted, ep_index)[:, None] * parts + jnp.arange(parts, dtype=jnp.int32)[None, :]
    ).reshape(-1)
    mine = (mine[:, None] * 2 + halves[None, :]).reshape(-1)
    named = (train_map[:, None] * 2 + halves[None, :]).reshape(-1)
    same = mine[:, None] == named[None, :]

    def picked(where):
        return jnp.sum(jnp.where(same, where[None, :], 0), axis=1)

    crossing = firsts[0] + place[6]
    tables = jnp.concatenate(
        [
            listed(flags[0], place[0], ROOM, where_low),
            listed(flags[1], place[1], ROOM, where_down),
            listed(flags[4], place[4], own, where_low + 1),
            listed(flags[6], crossing, ROOM, where_low),
            listed(flags[6], crossing, ROOM, where_high),
            picked(where_low),
            picked(where_high),
            picked(where_cross),
        ]
    ).astype(jnp.int32)
    return needed, tables


def stream_body(
    tokens, route_ids, route_weights, train_map, serve_place, train_gate, train_up, train_down
):
    ep_count = lax.axis_size("ep")
    tp_count = lax.axis_size("tp")
    ep_index = lax.axis_index("ep")
    slot_count = serve_place.shape[0]
    local, piece_rows, width = train_gate.shape
    parts = slot_count // EXPERTS
    step_count, tok_count, model_width = tokens.shape
    topk_count = route_ids.shape[2]
    rows = step_count * tok_count
    half = piece_rows // 2
    full = slot_count - 2 * local
    caps = [c for c in CAPS if c < full] + [full]

    slot_iota = jnp.arange(slot_count, dtype=jnp.int32)
    first = ~jnp.any(
        (serve_place[:, None] == serve_place[None, :]) & (slot_iota[None, :] < slot_iota[:, None]),
        axis=1,
    )
    holder = jnp.where(first, serve_place, -1)
    ids = route_ids.reshape(rows, topk_count)
    weights = route_weights.reshape(rows, topk_count)
    mix = jnp.sum(
        jnp.where(ids[:, :, None] == holder[None, None, :], weights[:, :, None], 0.0), axis=1
    )
    mix = mix.reshape(rows, ep_count, local).transpose(1, 0, 2)
    mix = jnp.pad(mix, ((0, 0), (0, 0), (0, 128 - local)))
    ordered = tokens.reshape(rows, model_width)
    needed, idx = routing(train_map, serve_place, ep_index, ep_count, local, parts)
    choice = sum((needed > c).astype(jnp.int32) for c in caps[:-1])
    trains = [t.reshape(2 * local, half, width) for t in (train_gate, train_up, train_down)]

    def run(collective, cap_static):
        def branch(idx, ordered, mix, *trains):
            return tuple(stream(idx, ordered, mix, trains, ep_count, local, cap_static, collective))

        return branch

    raw_gate, raw_up, raw_down, combined = lax.switch(
        choice, [run(k, c) for k, c in enumerate(caps)], idx, ordered, mix, *trains
    )
    raw_gate, raw_up, raw_down = (
        o.reshape(local, model_width, width) for o in (raw_gate, raw_up, raw_down)
    )
    blocks = 2 * parts // tp_count
    spread = lax.all_to_all(combined, "tp", split_axis=0, concat_axis=0, tiled=True)
    serve_gate, serve_up = move(raw_gate, raw_up)
    spread, serve_gate, serve_up = lax.optimization_barrier((spread, serve_gate, serve_up))
    spread = spread.reshape(tp_count, blocks, ep_count, rows, half).astype(jnp.float32)
    summed = jnp.sum(spread, axis=0).astype(jnp.bfloat16).transpose(1, 0, 2, 3)
    returned = lax.all_to_all(summed, "ep", split_axis=0, concat_axis=0, tiled=True)
    (serve_down,) = move(raw_down)
    returned, serve_down = lax.optimization_barrier((returned, serve_down))
    moe_out = jnp.sum(returned.astype(jnp.float32), axis=0).astype(jnp.bfloat16)
    moe_out = moe_out.transpose(1, 0, 2).reshape(
        step_count, tok_count, model_width // tp_count
    )
    return (serve_gate, serve_up, serve_down, moe_out)


def settle_kernel(source, target):
    target[...] = source[...]


def settle(source):
    slots, rows, width = source.shape
    spec = pl.BlockSpec((1, rows, width), lambda i: (i, 0, 0))
    return pl.pallas_call(
        settle_kernel,
        grid=(slots,),
        out_shape=jax.ShapeDtypeStruct(source.shape, source.dtype),
        in_specs=[spec],
        out_specs=spec,
        cost_estimate=pl.CostEstimate(
            flops=0, bytes_accessed=4 * slots * rows * width, transcendentals=0
        ),
    )(source)


def move_kernel(pieces, lag, count, *refs):
    sources, targets = refs[:count], refs[count : 2 * count]
    held, in_sem, out_sem = refs[2 * count :]
    deep, rows = held.shape[:2]
    total = count * pieces

    def piece(ref, i):
        return ref.at[pl.ds(pl.multiple_of(i * rows, rows), rows)]

    def each_array(n, action):
        for a in range(count):

            @pl.when((n >= a * pieces) & (n < (a + 1) * pieces))
            def _():
                action(a, n - a * pieces)

    def take(a, i, slot):
        return pltpu.make_async_copy(piece(sources[a], i), held.at[slot], in_sem.at[slot])

    def give(a, i, slot):
        return pltpu.make_async_copy(held.at[slot], piece(targets[a], i), out_sem.at[slot])

    def step(n, carry):
        @pl.when(n < total)
        def _():
            slot = lax.rem(n, deep)

            @pl.when(n >= deep)
            def _():
                give(0, 0, slot).wait()

            each_array(n, lambda a, i: take(a, i, slot).start())

        @pl.when(n >= lag)
        def _():
            slot = lax.rem(n - lag, deep)
            take(0, 0, slot).wait()
            each_array(n - lag, lambda a, i: give(a, i, slot).start())

        return carry

    lax.fori_loop(0, total + lag, step, 0)
    for slot in range(deep):
        give(0, 0, slot).wait()


def move(*arrays):
    slots, rows, width = arrays[0].shape
    flat = [a.reshape(slots * rows, width) for a in arrays]
    pieces, deep = 2 * slots, min(8, 2 * slots)
    any_spec = pl.BlockSpec(memory_space=pl.ANY)
    dma = pltpu.SemaphoreType.DMA
    moved = pl.pallas_call(
        functools.partial(move_kernel, pieces, deep // 2, len(flat)),
        out_shape=[jax.ShapeDtypeStruct(a.shape, a.dtype) for a in flat],
        in_specs=[any_spec] * len(flat),
        out_specs=[any_spec] * len(flat),
        scratch_shapes=[
            pltpu.VMEM((deep, rows // 2, width), flat[0].dtype),
            dma((deep,)),
            dma((deep,)),
        ],
        cost_estimate=pl.CostEstimate(
            flops=0, bytes_accessed=4 * len(flat) * slots * rows * width, transcendentals=0
        ),
        compiler_params=pltpu.CompilerParams(vmem_limit_bytes=48 * 2**20),
    )(*flat)
    return [a.reshape(slots, rows, width) for a in moved]


def solution(mesh):
    in_specs = (
        P(None, "ep", None),
        P(None, "ep", None),
        P(None, "ep", None),
        P(),
        P(),
        P("ep", None, "tp"),
        P("ep", None, "tp"),
        P("ep", None, "tp"),
    )
    out_specs = (P("ep", None, "tp"), P("ep", None, "tp"), P("ep", None, "tp"), P(None, "ep", "tp"))
    chosen = stream_body if mesh.shape["ep"] <= 8 else body
    return jax.shard_map(chosen, mesh=mesh, in_specs=in_specs, out_specs=out_specs, check_vma=False)
```
